512 devices in a mesh: group: 4 (over x), shard: 32 (over z, y_hi), tensor: 4 (over y_lo, core).
Axes of the slice: x: 4, y: 4 (y_hi: 2, y_lo: 2; y = y_hi * 2 + y_lo), z: 16, core: 2. Of those that a mesh axis runs over, the one named last changes fastest.
Arguments:
- deltas: bfloat16 [4, 2048, 2048], P('group', None, 'tensor'), may hold values from -6 to 6
- factor: bfloat16 [2048, 64], P('tensor'), may hold values from -0.29882812 to 0.29882812
- master: float32 [2048, 2048], P(('group', 'shard'), 'tensor'), may hold values from -6 to 6
- momentum: float32 [2048, 2048], P(('group', 'shard'), 'tensor'), may hold values from -3 to 3
Outputs:
- new_master: float32 [2048, 2048], P(('group', 'shard'), 'tensor')
- new_momentum: float32 [2048, 2048], P(('group', 'shard'), 'tensor')
- weights: bfloat16 [2048, 2048], P(None, 'tensor')
The draws below stay inside these ranges and needn't reach their ends.
All inputs are finite; a program needn't handle non-finite values.
Results may differ from the reference program's by a relative error of at most 0.009.
Values may be sent and summed in bfloat16 or wider, within the bound.
A program may use at most 64 MiB of HBM per device.

```python
import jax
import jax.numpy as jnp
from jax import lax

D = 2048
RANK = 64
GROUPS = 4
WIDTH_Q = 2048


def shard_levels(key, dims, shards, least, top_value):
    loudness = 1.0
    for position, parts in shards:
        heights = jax.random.uniform(jax.random.fold_in(jax.random.fold_in(key, 6), position), (parts,), jnp.float32, least / len(shards), top_value / len(shards))
        loudness = loudness * jnp.repeat(jnp.exp(heights), dims[position] // parts).reshape((-1,) + (1,) * (len(dims) - 1 - position))
    return loudness


def gaussian(key, shape, spread, limit, cuts=(), kind=jnp.bfloat16):
    factor_of = shard_levels(key, shape, cuts, -0.22, 0.18) if cuts else 1.0
    entries = jax.random.normal(key, shape, jnp.float32) * spread * factor_of
    return jnp.minimum(jnp.maximum(entries, -limit), limit).astype(kind)


def setup_inputs(seed: int = 0) -> dict:
    streams_of = jax.random.split(jax.random.key(seed), 5)
    deltas = gaussian(streams_of[0], (GROUPS, D, WIDTH_Q), 1.0, 6.0, ((0, 4), (2, 4)))
    factor = gaussian(streams_of[1], (WIDTH_Q, RANK), 0.05, 0.29882812, ((0, 4),))
    master = gaussian(streams_of[2], (D, WIDTH_Q), 1.0, 6.0, ((0, 128), (1, 4)), jnp.float32)
    momentum = gaussian(streams_of[3], (D, WIDTH_Q), 0.5, 3.0, ((0, 128), (1, 4)), jnp.float32)
    return {"deltas": deltas, "factor": factor, "master": master, "momentum": momentum}


momentum_rate = 0.9
outer_rate = 0.7


def reference(deltas, factor, master, momentum):
    coefficients = jnp.zeros((D, RANK), jnp.float32)
    for group_number in range(GROUPS):
        coefficients = coefficients + jnp.dot(deltas[group_number], factor, preferred_element_type=jnp.float32)
    factor_wide = factor.astype(jnp.float32)
    outer_grad = lax.dot_general(coefficients, factor_wide, (((1,), (1,)), ((), ())), precision=lax.Precision.HIGHEST) / GROUPS
    new_momentum = momentum_rate * momentum + outer_grad
    new_master = master - outer_rate * (outer_grad + momentum_rate * new_momentum)
    return new_master, new_momentum, new_master.astype(jnp.bfloat16)
```

```python
import jax
import jax.numpy as jnp
from jax import lax
from jax.experimental import pallas as pl
from jax.experimental.pallas import tpu as pltpu
from jax.sharding import PartitionSpec as P

momentum_rate = 0.9
outer_rate = 0.7
MESH = pl.DeviceIdType.MESH


def kernel(
    deltas_ref, factor_ref, master_ref, momentum_ref,
    new_master_ref, new_momentum_ref, weights_ref,
    delta, factor, master, momentum, partial, incoming, new_master, new_momentum, full,
    in_sem, out_sem, full_sem, sum_send, sum_recv, plane_send, plane_recv, ring_send, ring_recv,
):
    groups, depth = full.shape[0], full.shape[1]
    tensors = lax.axis_size("tensor")
    g, s, t = lax.axis_index("group"), lax.axis_index("shard"), lax.axis_index("tensor")
    z, y = s // 2, s % 2
    rows = master.shape[0]
    half = rows // 2
    rank = factor.shape[0]

    loads = [
        pltpu.make_async_copy(deltas_ref.at[:, s], delta, in_sem.at[0]),
        pltpu.make_async_copy(factor_ref, factor, in_sem.at[1]),
        pltpu.make_async_copy(master_ref, master, in_sem.at[2]),
        pltpu.make_async_copy(momentum_ref, momentum, in_sem.at[3]),
    ]
    for load in loads:
        load.start()

    def around(value, step, size):
        return lax.rem(value + step + size, size)

    def device(dg, dy, dz, dt):
        shard = around(z, dz, depth) * 2 + around(y, dy, 2)
        return (around(g, dg, groups), shard, around(t, dt, tensors))

    sums = [(dg, dt) for dg in range(groups) for dt in range(tensors) if dg or dt]
    planes = [(dg, dy) for dg in range(groups) for dy in range(2) if dg or dy]
    peers = [(dg, 0, 0, dt) for dg, dt in sums]
    peers += [(dg, 1, 0, 0) for dg in range(groups)]
    peers += [(0, 0, 1, 0), (0, 0, -1, 0)]
    barrier = pltpu.get_barrier_semaphore()
    for peer in peers:
        pl.semaphore_signal(barrier, inc=1, device_id=device(*peer), device_id_type=MESH)

    loads[0].wait()
    loads[1].wait()
    part = lax.dot_general(
        delta[...].reshape(groups * rows, delta.shape[2]), factor[...], (((1,), (1,)), ((), ())),
        preferred_element_type=jnp.float32,
    )
    for i in range(groups):
        partial[i] = jnp.concatenate(
            [part[i * rows : i * rows + half], part[i * rows + half : (i + 1) * rows]], axis=1
        )

    pl.semaphore_wait(barrier, len(peers))

    copies = []
    for i, (dg, dt) in enumerate(sums):
        target = device(dg, 0, 0, dt)
        copy = pltpu.make_async_remote_copy(
            src_ref=partial.at[target[0]], dst_ref=incoming.at[i],
            send_sem=sum_send.at[i], recv_sem=sum_recv.at[i],
            device_id=target, device_id_type=MESH,
        )
        copy.start()
        copies.append(copy)
    loads[2].wait()
    loads[3].wait()
    total = partial[g]
    for i, copy in enumerate(copies):
        copy.wait_recv()
        total = total + incoming[i]
    coefficients = jnp.concatenate([total[:, :rank], total[:, rank:]], axis=0)
    outer_grad = lax.dot_general(
        coefficients, factor[...].astype(jnp.float32), (((1,), (0,)), ((), ())),
        precision=lax.Precision.HIGHEST, preferred_element_type=jnp.float32,
    ) / groups
    moved = momentum_rate * momentum[...] + outer_grad
    updated = master[...] - outer_rate * (outer_grad + momentum_rate * moved)
    fresh = updated.astype(jnp.bfloat16)
    full[g, z, y] = fresh

    plane_copies = {}
    for i, (dg, dy) in enumerate(planes):
        copy = pltpu.make_async_remote_copy(
            src_ref=full.at[g, z, y], dst_ref=full.at[g, z, y],
            send_sem=plane_send.at[i], recv_sem=plane_recv.at[i],
            device_id=device(dg, dy, 0, 0), device_id_type=MESH,
        )
        copy.start()
        plane_copies[dg, dy] = copy
    new_momentum[...] = moved
    new_master[...] = updated
    stores = [
        pltpu.make_async_copy(new_master, new_master_ref, out_sem.at[0]),
        pltpu.make_async_copy(new_momentum, new_momentum_ref, out_sem.at[1]),
    ]
    for store in stores:
        store.start()

    ring_copies = []

    def send(way, k, dg, block):
        copy = pltpu.make_async_remote_copy(
            src_ref=block, dst_ref=block,
            send_sem=ring_send.at[way, k, dg], recv_sem=ring_recv.at[way, k, dg],
            device_id=device(0, 0, 1 - 2 * way, 0), device_id_type=MESH,
        )
        copy.start()
        ring_copies.append(copy)

    def keep(block, g_of, z_of):
        pltpu.make_async_copy(block, weights_ref.at[g_of, z_of], full_sem).start()

    steps = depth // 2

    def last(way, dg):
        return (dg < groups // 2) == (way == 0)

    for dg in range(groups):
        g_of = around(g, -dg, groups)
        for dy in range(2):
            if dg or dy:
                plane_copies[dg, dy].wait_recv()
        block = full.at[g_of, z]
        for way in range(2):
            send(way, 0, dg, block)
        keep(block, g_of, z)
    for k in range(1, steps + 1):
        for dg in range(groups):
            g_of = around(g, -dg, groups)
            for way in range(2):
                if k == steps and not last(way, dg):
                    continue
                z_of = around(z, k if way else -k, depth)
                block = full.at[g_of, z_of]
                pltpu.make_async_remote_copy(
                    src_ref=block, dst_ref=block,
                    send_sem=ring_send.at[way, k - 1, dg], recv_sem=ring_recv.at[way, k - 1, dg],
                    device_id=device(0, 0, 1 - 2 * way, 0), device_id_type=MESH,
                ).wait_recv()
                if k < steps - 1 or (k == steps - 1 and last(way, dg)):
                    send(way, k, dg, block)
                keep(block, g_of, z_of)

    for copy in copies:
        copy.wait_send()
    for copy in plane_copies.values():
        copy.wait_send()
    for copy in ring_copies:
        copy.wait_send()
    for store in stores:
        store.wait()
    pltpu.make_async_copy(full, weights_ref, full_sem).wait()


def shards(deltas, factor, master, momentum):
    groups = lax.axis_size("group")
    tensors = lax.axis_size("tensor")
    depth = lax.axis_size("shard") // 2
    rows, cols = master.shape
    rank = factor.shape[1]
    steps = depth // 2
    hbm = pl.BlockSpec(memory_space=pl.ANY)
    dma = pltpu.SemaphoreType.DMA
    full = (groups, depth, 2, rows, cols)
    new_master, new_momentum, weights = pl.pallas_call(
        kernel,
        out_shape=(
            jax.ShapeDtypeStruct(master.shape, jnp.float32),
            jax.ShapeDtypeStruct(momentum.shape, jnp.float32),
            jax.ShapeDtypeStruct(full, jnp.bfloat16),
        ),
        in_specs=[hbm] * 4,
        out_specs=(hbm,) * 3,
        scratch_shapes=[
            pltpu.VMEM((groups, rows, cols), jnp.bfloat16),
            pltpu.VMEM((rank, cols), jnp.bfloat16),
            pltpu.VMEM((rows, cols), jnp.float32),
            pltpu.VMEM((rows, cols), jnp.float32),
            pltpu.VMEM((groups, rows // 2, 2 * rank), jnp.float32),
            pltpu.VMEM((groups * tensors - 1, rows // 2, 2 * rank), jnp.float32),
            pltpu.VMEM((rows, cols), jnp.float32),
            pltpu.VMEM((rows, cols), jnp.float32),
            pltpu.VMEM(full, jnp.bfloat16),
            dma((4,)), dma((2,)), dma,
            dma((groups * tensors - 1,)), dma((groups * tensors - 1,)),
            dma((groups * 2 - 1,)), dma((groups * 2 - 1,)),
            dma((2, steps, groups)), dma((2, steps, groups)),
        ],
        compiler_params=pltpu.CompilerParams(collective_id=0, has_side_effects=True),
    )(deltas.reshape(groups, 2 * depth, rows, cols), factor.T, master, momentum)
    return new_master, new_momentum, weights.reshape(groups * depth * 2 * rows, cols)


def solution(mesh):
    return jax.shard_map(
        shards,
        mesh=mesh,
        in_specs=(
            P("group", None, "tensor"),
            P("tensor", None),
            P(("group", "shard"), "tensor"),
            P(("group", "shard"), "tensor"),
        ),
        out_specs=(
            P(("group", "shard"), "tensor"),
            P(("group", "shard"), "tensor"),
            P(None, "tensor"),
        ),
        check_vma=False,
    )
```

```python
import jax
import jax.numpy as jnp
from jax import lax
from jax.experimental import pallas as pl
from jax.experimental.pallas import tpu as pltpu
from jax.sharding import PartitionSpec as P

momentum_rate = 0.9
outer_rate = 0.7
MESH = pl.DeviceIdType.MESH
AROUND = (1, -1, 2)


def kernel(
    deltas_ref, factor_ref, master_ref, momentum_ref,
    new_master, new_momentum, full,
    delta, factor, master, momentum, partial, incoming,
    in_sem, sum_send, sum_recv, far_send, far_recv, y_send, y_recv,
    mid_send, mid_recv, last_send, last_recv, pass_send, pass_recv,
):
    groups, zhs, zls = full.shape[:3]
    tensors = lax.axis_size("tensor")
    g, s, t = lax.axis_index("group"), lax.axis_index("shard"), lax.axis_index("tensor")
    z, y = s // 2, s % 2
    depth = zhs * zls
    rows = master.shape[0]
    half = rows // 2
    rank = factor.shape[0]

    loads = [
        pltpu.make_async_copy(deltas_ref.at[:, s], delta, in_sem.at[0]),
        pltpu.make_async_copy(factor_ref, factor, in_sem.at[1]),
        pltpu.make_async_copy(master_ref, master, in_sem.at[2]),
        pltpu.make_async_copy(momentum_ref, momentum, in_sem.at[3]),
    ]
    for load in loads:
        load.start()

    def around(value, step, size):
        return lax.rem(value + step + size, size)

    def device(dg, dy, dz, dt):
        shard = around(z, dz, depth) * 2 + around(y, dy, 2)
        return (around(g, dg, groups), shard, around(t, dt, tensors))

    sums = [(dg, dt) for dg in range(groups) for dt in range(tensors) if dg or dt]
    peers = [(dg, 0, 0, dt) for dg, dt in sums] + [(0, 1, 0, 0)]
    peers += [(0, 0, dz, 0) for dz in (1, -1, 2, -2, zls, -zls, 2 * zls)]
    barrier = pltpu.get_barrier_semaphore()
    for peer in peers:
        pl.semaphore_signal(barrier, inc=1, device_id=device(*peer), device_id_type=MESH)

    loads[0].wait()
    loads[1].wait()
    part = lax.dot_general(
        delta[...].reshape(groups * rows, delta.shape[2]), factor[...], (((1,), (1,)), ((), ())),
        preferred_element_type=jnp.float32,
    )
    for i in range(groups):
        partial[i] = jnp.concatenate(
            [part[i * rows : i * rows + half], part[i * rows + half : (i + 1) * rows]], axis=1
        )

    pl.semaphore_wait(barrier, len(peers))

    sent = []

    def copy(block, send_sem, recv_sem, target, into=None):
        return pltpu.make_async_remote_copy(
            src_ref=block, dst_ref=block if into is None else into,
            send_sem=send_sem, recv_sem=recv_sem, device_id=target, device_id_type=MESH,
        )

    def send(*args):
        move = copy(*args)
        move.start()
        sent.append(move)

    for i, (dg, dt) in enumerate(sums):
        target = device(dg, 0, 0, dt)
        send(partial.at[target[0]], sum_send.at[i], sum_recv.at[i], target, incoming.at[i])
    loads[2].wait()
    loads[3].wait()
    total = partial[g]
    for i in range(len(sums)):
        sent[i].wait_recv()
        total = total + incoming[i]
    coefficients = jnp.concatenate([total[:, :rank], total[:, rank:]], axis=0)
    outer_grad = lax.dot_general(
        coefficients, factor[...].astype(jnp.float32), (((1,), (0,)), ((), ())),
        precision=lax.Precision.HIGHEST, preferred_element_type=jnp.float32,
    ) / groups
    moved = momentum_rate * momentum[...] + outer_grad
    updated = master[...] - outer_rate * (outer_grad + momentum_rate * moved)

    def places(z_of):
        zh, zl = z_of // zls, lax.rem(z_of, zls)
        return [zh] + [around(zh, -d, zhs) for d in AROUND], zl

    zh_mine, zl = places(z)
    here = full.at[g, zh_mine[0], zl, y]
    here[0] = updated[:half].astype(jnp.bfloat16)
    here[1] = updated[half:].astype(jnp.bfloat16)

    def far(i):
        return full.at[g, zh_mine[i], zl, y]

    def over_y(i):
        send(far(i), y_send.at[i], y_recv.at[i], device(0, 1, 0, 0))

    def wait(block, send_sem, recv_sem):
        copy(block, send_sem, recv_sem, device(0, 1, 0, 0)).wait_recv()

    for i, d in enumerate(AROUND):
        send(here, far_send.at[i], far_recv.at[i], device(0, 0, d * zls, 0))
    over_y(0)
    new_momentum[...] = moved
    new_master[...] = updated

    def hop(axis, d):
        return device(d, 0, 0, 0) if axis == 0 else device(0, 0, d, 0)

    def mid(i):
        wait(full.at[g, zh_mine[i], zl, 1 - y], y_send.at[i], y_recv.at[i])
        for part in range(2):
            block = full.at[g, zh_mine[i], zl, :, part]
            for j, d in enumerate(AROUND):
                send(block, mid_send.at[part, j, i], mid_recv.at[part, j, i], hop(part, d))

    for i in range(1, 3):
        wait(far(i), far_send.at[i - 1], far_recv.at[i - 1])
        over_y(i)
    mid(0)
    wait(far(3), far_send.at[2], far_recv.at[2])
    over_y(3)
    for i in range(1, 4):
        mid(i)

    def chunk(part, u, w):
        if part == 0:
            return full.at[around(g, -u, groups), :, around(zl, -w, zls), :, 0]
        return full.at[around(g, -w, groups), :, around(zl, -u, zls), :, 1]

    froms = (0,) + AROUND
    for j, d in enumerate(froms):
        for part in range(2):
            if j:
                for i in range(4):
                    if part == 0:
                        block = full.at[around(g, -d, groups), zh_mine[i], zl, :, 0]
                    else:
                        zh_of, zl_of = places(around(z, -d, depth))
                        block = full.at[g, zh_of[i], zl_of, :, 1]
                    wait(block, mid_send.at[part, j - 1, i], mid_recv.at[part, j - 1, i])
            for way in range(2):
                send(
                    chunk(part, d, 0), last_send.at[part, way, j], last_recv.at[part, way, j],
                    hop(1 - part, 1 - 2 * way),
                )
    for j, d in enumerate(froms):
        for part in range(2):
            for way in range(2):
                block = chunk(part, d, 1 - 2 * way)
                wait(block, last_send.at[part, way, j], last_recv.at[part, way, j])
                if j % 2 == way:
                    send(block, pass_send.at[part, j], pass_recv.at[part, j], hop(1 - part, 1 - 2 * way))
    for j, d in enumerate(froms):
        for part in range(2):
            wait(chunk(part, d, 2), pass_send.at[part, j], pass_recv.at[part, j])
    for move in sent:
        move.wait_send()


def store(*refs):
    sem = refs[-1]
    count = len(refs) // 2
    moves = [pltpu.make_async_copy(refs[i], refs[count + i], sem.at[i]) for i in range(count)]
    for move in moves:
        move.start()
    for move in moves:
        move.wait()


def shards(deltas, factor, master, momentum):
    groups = lax.axis_size("group")
    tensors = lax.axis_size("tensor")
    depth = lax.axis_size("shard") // 2
    rows, cols = master.shape
    rank = factor.shape[1]
    anywhere = pl.BlockSpec(memory_space=pl.ANY)
    vmem = pl.BlockSpec(memory_space=pltpu.VMEM)
    dma = pltpu.SemaphoreType.DMA
    full = (groups, 4, depth // 4, 2, 2, rows // 2, cols)
    results = pl.pallas_call(
        kernel,
        out_shape=(
            pltpu.VMEM(master.shape, jnp.float32),
            pltpu.VMEM(momentum.shape, jnp.float32),
            pltpu.VMEM(full, jnp.bfloat16),
        ),
        in_specs=[anywhere] * 4,
        out_specs=(vmem,) * 3,
        scratch_shapes=[
            pltpu.VMEM((groups, rows, cols), jnp.bfloat16),
            pltpu.VMEM((rank, cols), jnp.bfloat16),
            pltpu.VMEM((rows, cols), jnp.float32),
            pltpu.VMEM((rows, cols), jnp.float32),
            pltpu.VMEM((groups, rows // 2, 2 * rank), jnp.float32),
            pltpu.VMEM((groups * tensors - 1, rows // 2, 2 * rank), jnp.float32),
            dma((4,)), dma((groups * tensors - 1,)), dma((groups * tensors - 1,)),
            dma((3,)), dma((3,)), dma((4,)), dma((4,)),
            dma((2, 3, 4)), dma((2, 3, 4)), dma((2, 2, 4)), dma((2, 2, 4)), dma((2, 4)), dma((2, 4)),
        ],
        compiler_params=pltpu.CompilerParams(collective_id=0, has_side_effects=True),
    )(deltas.reshape(groups, 2 * depth, rows, cols), factor.T, master, momentum)
    new_master, new_momentum, weights = pl.pallas_call(
        store,
        out_shape=tuple(jax.ShapeDtypeStruct(r.shape, r.dtype) for r in results),
        in_specs=[anywhere] * 3,
        out_specs=(anywhere,) * 3,
        scratch_shapes=[dma((3,))],
        compiler_params=pltpu.CompilerParams(vmem_limit_bytes=1 << 20),
    )(*results)
    return new_master, new_momentum, weights.reshape(groups * depth * 2 * rows, cols)


def solution(mesh):
    return jax.shard_map(
        shards,
        mesh=mesh,
        in_specs=(
            P("group", None, "tensor"),
            P("tensor", None),
            P(("group", "shard"), "tensor"),
            P(("group", "shard"), "tensor"),
        ),
        out_specs=(
            P(("group", "shard"), "tensor"),
            P(("group", "shard"), "tensor"),
            P(None, "tensor"),
        ),
        check_vma=False,
    )
```

```python
import jax
import jax.numpy as jnp
from jax import lax
from jax.experimental import pallas as pl
from jax.experimental.pallas import tpu as pltpu
from jax.sharding import PartitionSpec as P

momentum_rate = 0.9
outer_rate = 0.7
MESH = pl.DeviceIdType.MESH
AROUND = (1, -1, 2)


def kernel(
    deltas_ref, factor_ref, master_ref, momentum_ref,
    new_master, new_momentum, full,
    delta, factor, master, momentum, partial, incoming, base, grad,
    in_sem, sum_send, sum_recv, far_send, far_recv, y_send, y_recv,
    mid_send, mid_recv, last_send, last_recv, pass_send, pass_recv,
):
    groups, zls = full.shape[0], full.shape[3]
    zhs = full.shape[1] * full.shape[2]
    tensors = lax.axis_size("tensor")
    g, s, t = lax.axis_index("group"), lax.axis_index("shard"), lax.axis_index("tensor")
    z, y = s // 2, s % 2
    depth = zhs * zls
    rows = master.shape[0]
    half = rows // 2
    rank = factor.shape[0]

    def around(value, step, size):
        return lax.rem(value + step + size, size)

    def device(dg, dy, dz, dt):
        shard = around(z, dz, depth) * 2 + around(y, dy, 2)
        return (around(g, dg, groups), shard, around(t, dt, tensors))

    def place(dz):
        other = around(z, dz, depth)
        return other // zls, lax.rem(other, zls)

    zh, zl = place(0)
    loads = [
        pltpu.make_async_copy(deltas_ref.at[:, :, zl, y], delta, in_sem.at[0]),
        pltpu.make_async_copy(factor_ref, factor, in_sem.at[1]),
        pltpu.make_async_copy(master_ref, master, in_sem.at[2]),
        pltpu.make_async_copy(momentum_ref, momentum, in_sem.at[3]),
    ]
    for load in loads:
        load.start()

    sums = [(dg, dt) for dg in range(groups) for dt in range(tensors) if dg or dt]
    peers = [(dg, 0, 0, dt) for dg, dt in sums] + [(0, 1, 0, 0)]
    peers += [(0, 0, dz, 0) for dz in (1, -1, 2, -2, zls, -zls)]
    barrier = pltpu.get_barrier_semaphore()
    for peer in peers:
        pl.semaphore_signal(barrier, inc=1, device_id=device(*peer), device_id_type=MESH)

    loads[2].wait()
    loads[3].wait()
    start = master[...] - outer_rate * momentum_rate * momentum_rate * momentum[...]
    mine = base.at[zh // 2, zh % 2]
    mine[0] = start[:half]
    mine[1] = start[half:]
    loads[0].wait()
    loads[1].wait()
    span = zhs * rows
    part = lax.dot_general(
        delta[...].reshape(groups * span, delta.shape[-1]), factor[...], (((1,), (1,)), ((), ())),
        preferred_element_type=jnp.float32,
    )
    for i in range(groups):
        own = part[i * span : (i + 1) * span]
        partial[i] = jnp.concatenate([own[: span // 2], own[span // 2 :]], axis=1)

    pl.semaphore_wait(barrier, len(peers))

    sent = []

    def copy(block, send_sem, recv_sem, target, into=None):
        return pltpu.make_async_remote_copy(
            src_ref=block, dst_ref=block if into is None else into,
            send_sem=send_sem, recv_sem=recv_sem, device_id=target, device_id_type=MESH,
        )

    def send(*args):
        move = copy(*args)
        move.start()
        sent.append(move)

    def wait(block, send_sem, recv_sem):
        copy(block, send_sem, recv_sem, device(0, 1, 0, 0)).wait_recv()

    def start_of(step):
        other = around(zh, step, zhs)
        return base.at[other // 2, other % 2]

    for way in range(2):
        send(mine, far_send.at[way], far_recv.at[way], device(0, 0, zls * (1 - 2 * way), 0))
    for i, (dg, dt) in enumerate(sums):
        target = device(dg, 0, 0, dt)
        send(partial.at[target[0]], sum_send.at[i], sum_recv.at[i], target, incoming.at[i])
    for way in range(2):
        block = start_of(2 * way - 1)
        wait(block, far_send.at[way], far_recv.at[way])
        send(
            block.at[way], far_send.at[2 + way], far_recv.at[2 + way],
            device(0, 0, zls * (1 - 2 * way), 0),
        )

    total = partial[g]
    for i in range(len(sums)):
        sent[2 + i].wait_recv()
        total = total + incoming[i]
    coefficients = jnp.concatenate([total[:, :rank], total[:, rank:]], axis=0)
    outer_grad = lax.dot_general(
        coefficients, factor[...].astype(jnp.float32), (((1,), (0,)), ((), ())),
        precision=lax.Precision.HIGHEST, preferred_element_type=jnp.float32,
    ) / groups
    grad[...] = outer_grad.reshape(grad.shape)

    def pair(k, dz=0):
        zh_of, zl_of = place(dz)
        return (zh_of + 1 - k) % 2, zl_of

    def finish(k):
        parity = pair(k)[0]
        fresh = base[:, parity] - outer_rate * (1 + momentum_rate) * grad[:, parity]
        full[g, :, parity, zl, y] = fresh.astype(jnp.bfloat16)
        send(full.at[g, :, parity, zl, y], y_send.at[k], y_recv.at[k], device(0, 1, 0, 0))

    def hop(axis, d):
        return device(d, 0, 0, 0) if axis == 0 else device(0, 0, d, 0)

    def block(part, u, w, k, o):
        dg, dz = (u, w) if part == 0 else (w, u)
        parity, zl_of = pair(k, -dz)
        return full.at[around(g, -dg, groups), :, parity, zl_of, y if o == 0 else 1 - y, part]

    froms = (0,) + AROUND

    def last(part, j, k, o):
        for way in range(2):
            send(
                block(part, froms[j], 0, k, o), last_send.at[part, way, j, k, o],
                last_recv.at[part, way, j, k, o], hop(1 - part, 1 - 2 * way),
            )

    def begin(k, o):
        if o:
            wait(full.at[g, :, pair(k)[0], zl, 1 - y], y_send.at[k], y_recv.at[k])
        for j, d in enumerate(AROUND):
            for part in range(2):
                send(
                    block(part, 0, 0, k, o), mid_send.at[part, j, k, o], mid_recv.at[part, j, k, o],
                    hop(part, d),
                )
        for part in range(2):
            last(part, 0, k, o)

    def middle(j, k, o):
        for part in range(2):
            wait(
                block(part, froms[j], 0, k, o), mid_send.at[part, j - 1, k, o], mid_recv.at[part, j - 1, k, o]
            )
            last(part, j, k, o)

    def onward(j, k, o):
        for part in range(2):
            for way in range(2):
                came = block(part, froms[j], 1 - 2 * way, k, o)
                wait(came, last_send.at[part, way, j, k, o], last_recv.at[part, way, j, k, o])
                if j % 2 == way:
                    send(
                        came, pass_send.at[part, j, k, o], pass_recv.at[part, j, k, o],
                        hop(1 - part, 1 - 2 * way),
                    )

    def ended(j, k, o):
        for part in range(2):
            came = block(part, froms[j], 2 - 4 * (j % 2), k, o)
            wait(came, pass_send.at[part, j, k, o], pass_recv.at[part, j, k, o])

    finish(0)
    begin(0, 0)
    moved = momentum_rate * momentum[...]
    own = grad.at[zh // 2, zh % 2]
    for i in range(2):
        new_momentum[i * half : (i + 1) * half] = moved[i * half : (i + 1) * half] + own[i]
        new_master[i * half : (i + 1) * half] = mine[i] - outer_rate * (1 + momentum_rate) * own[i]
    for j in (1, 2):
        middle(j, 0, 0)
    for way in range(2):
        wait(start_of(2).at[way], far_send.at[2 + way], far_recv.at[2 + way])
    finish(1)
    begin(1, 0)
    onward(0, 0, 0)
    begin(0, 1)
    middle(3, 0, 0)
    onward(1, 0, 0)
    onward(2, 0, 0)
    middle(1, 1, 0)
    middle(2, 1, 0)
    begin(1, 1)
    onward(0, 1, 0)
    middle(1, 0, 1)
    middle(2, 0, 1)
    onward(0, 0, 1)
    onward(3, 0, 0)
    middle(3, 1, 0)
    middle(3, 0, 1)
    onward(1, 1, 0)
    onward(2, 1, 0)
    middle(1, 1, 1)
    middle(2, 1, 1)
    onward(1, 0, 1)
    onward(2, 0, 1)
    onward(0, 1, 1)
    onward(3, 1, 0)
    onward(3, 0, 1)
    middle(3, 1, 1)
    onward(1, 1, 1)
    onward(2, 1, 1)
    onward(3, 1, 1)
    for o in range(2):
        for k in range(2):
            for j in range(4):
                ended(j, k, o)
    for move in sent:
        move.wait_send()


def store(*refs):
    sem = refs[-1]
    count = len(refs) // 2
    moves = [pltpu.make_async_copy(refs[i], refs[count + i], sem.at[i]) for i in range(count)]
    for move in moves:
        move.start()
    for move in moves:
        move.wait()


def shards(deltas, factor, master, momentum):
    groups = lax.axis_size("group")
    tensors = lax.axis_size("tensor")
    depth = lax.axis_size("shard") // 2
    rows, cols = master.shape
    rank = factor.shape[1]
    anywhere = pl.BlockSpec(memory_space=pl.ANY)
    vmem = pl.BlockSpec(memory_space=pltpu.VMEM)
    dma = pltpu.SemaphoreType.DMA
    zls = depth // 4
    full = (groups, 2, 2, zls, 2, 2, rows // 2, cols)
    four = (2, 2, 2, rows // 2, cols)
    results = pl.pallas_call(
        kernel,
        out_shape=(
            pltpu.VMEM(master.shape, jnp.float32),
            pltpu.VMEM(momentum.shape, jnp.float32),
            pltpu.VMEM(full, jnp.bfloat16),
        ),
        in_specs=[anywhere] * 4,
        out_specs=(vmem,) * 3,
        scratch_shapes=[
            pltpu.VMEM((groups, 4, rows, cols), jnp.bfloat16),
            pltpu.VMEM((rank, cols), jnp.bfloat16),
            pltpu.VMEM((rows, cols), jnp.float32),
            pltpu.VMEM((rows, cols), jnp.float32),
            pltpu.VMEM((groups, 2 * rows, 2 * rank), jnp.float32),
            pltpu.VMEM((groups * tensors - 1, 2 * rows, 2 * rank), jnp.float32),
            pltpu.VMEM(four, jnp.float32),
            pltpu.VMEM(four, jnp.float32),
            dma((4,)), dma((groups * tensors - 1,)), dma((groups * tensors - 1,)),
            dma((4,)), dma((4,)), dma((2,)), dma((2,)),
            dma((2, 3, 2, 2)), dma((2, 3, 2, 2)), dma((2, 2, 4, 2, 2)), dma((2, 2, 4, 2, 2)),
            dma((2, 4, 2, 2)), dma((2, 4, 2, 2)),
        ],
        compiler_params=pltpu.CompilerParams(collective_id=0, has_side_effects=True),
    )(deltas.reshape(groups, 4, zls, 2, rows, cols), factor.T, master, momentum)
    new_master, new_momentum, weights = pl.pallas_call(
        store,
        out_shape=tuple(jax.ShapeDtypeStruct(r.shape, r.dtype) for r in results),
        in_specs=[anywhere] * 3,
        out_specs=(anywhere,) * 3,
        scratch_shapes=[dma((3,))],
        compiler_params=pltpu.CompilerParams(vmem_limit_bytes=1 << 20),
    )(*results)
    return new_master, new_momentum, weights.reshape(groups * depth * 2 * rows, cols)


def solution(mesh):
    return jax.shard_map(
        shards,
        mesh=mesh,
        in_specs=(
            P("group", None, "tensor"),
            P("tensor", None),
            P(("group", "shard"), "tensor"),
            P(("group", "shard"), "tensor"),
        ),
        out_specs=(
            P(("group", "shard"), "tensor"),
            P(("group", "shard"), "tensor"),
            P(None, "tensor"),
        ),
        check_vma=False,
    )
```

```python
import jax
import jax.numpy as jnp
from jax import lax
from jax.experimental import pallas as pl
from jax.experimental.pallas import tpu as pltpu
from jax.sharding import PartitionSpec as P

momentum_rate = 0.9
outer_rate = 0.7
MESH = pl.DeviceIdType.MESH
AROUND = (1, -1, 2)


def kernel(
    deltas_ref, factor_ref, master_ref, momentum_ref,
    new_master, new_momentum, full,
    delta, factor, master, momentum, partial, incoming, base, grad,
    in_sem, sum_send, sum_recv, far_send, far_recv, y_send, y_recv,
    mid_send, mid_recv, last_send, last_recv, end_send, end_recv,
):
    groups, zhs, zls = full.shape[:3]
    tensors = lax.axis_size("tensor")
    g, s, t = lax.axis_index("group"), lax.axis_index("shard"), lax.axis_index("tensor")
    z, y = s // 2, s % 2
    depth = zhs * zls
    rows = master.shape[0]
    half = rows // 2
    rank = factor.shape[0]

    def around(value, step, size):
        return lax.rem(value + step + size, size)

    def device(dg, dy, dz, dt):
        shard = around(z, dz, depth) * 2 + around(y, dy, 2)
        return (around(g, dg, groups), shard, around(t, dt, tensors))

    zh, zl = z // zls, lax.rem(z, zls)
    loads = [
        pltpu.make_async_copy(master_ref, master, in_sem.at[0]),
        pltpu.make_async_copy(momentum_ref, momentum, in_sem.at[1]),
        pltpu.make_async_copy(deltas_ref.at[:, :, zl, y], delta, in_sem.at[2]),
        pltpu.make_async_copy(factor_ref, factor, in_sem.at[3]),
    ]
    for load in loads:
        load.start()

    sums = [(dg, dt) for dg in (2, 1, -1, 0) for dt in (2, 1, -1, 0) if dg or dt]
    peers = [(0, 0, dz, 0) for dz in (zls, -zls)]
    peers += [(0, dy, dz, 0) for dz in (2, -2, 1, -1) for dy in range(2)]
    peers += [(dg, 1, 0, 0) for dg in (2, 1, -1, 0)]
    peers += [(dg, 0, 0, dt) for dg, dt in sums]
    barrier = pltpu.get_barrier_semaphore()
    for peer in peers:
        pl.semaphore_signal(barrier, inc=1, device_id=device(*peer), device_id_type=MESH)

    loads[0].wait()
    loads[1].wait()
    start = master[...] - outer_rate * momentum_rate * momentum_rate * momentum[...]
    mine = base.at[zh]
    mine[0] = start[:half]
    mine[1] = start[half:]
    loads[2].wait()
    loads[3].wait()
    span = zhs * rows
    part = lax.dot_general(
        delta[...].reshape(groups * span, delta.shape[-1]), factor[...], (((1,), (1,)), ((), ())),
        preferred_element_type=jnp.float32,
    )
    for i in range(groups):
        own = part[i * span : (i + 1) * span]
        partial[i] = jnp.concatenate([own[: span // 2], own[span // 2 :]], axis=1)

    pl.semaphore_wait(barrier, len(peers))

    def copy(block, send_sem, recv_sem, target, into=None):
        return pltpu.make_async_remote_copy(
            src_ref=block, dst_ref=block if into is None else into,
            send_sem=send_sem, recv_sem=recv_sem, device_id=target, device_id_type=MESH,
        )

    def wait(block, send_sem, recv_sem):
        copy(block, send_sem, recv_sem, device(0, 1, 0, 0)).wait_recv()

    def wait_sent(block, send_sem):
        copy(block, send_sem, end_recv, device(0, 1, 0, 0)).wait_send()

    for way in range(2):
        copy(mine, far_send, far_recv.at[way], device(0, 0, zls * (1 - 2 * way), 0)).start()
    for i, (dg, dt) in enumerate(sums):
        target = device(dg, 0, 0, dt)
        copy(partial.at[target[0]], sum_send, sum_recv, target, incoming.at[i]).start()
    for way in range(2):
        block = base.at[around(zh, 2 * way - 1, zhs)]
        wait(block, far_send, far_recv.at[way])
        copy(
            block.at[way], far_send, far_recv.at[2 + way], device(0, 0, zls * (1 - 2 * way), 0)
        ).start()

    wait(incoming, sum_send, sum_recv)
    total = partial[g]
    for i in range(len(sums)):
        total = total + incoming[i]
    coefficients = jnp.concatenate([total[:, :rank], total[:, rank:]], axis=0)
    outer_grad = lax.dot_general(
        coefficients, factor[...].astype(jnp.float32), (((1,), (0,)), ((), ())),
        precision=lax.Precision.HIGHEST, preferred_element_type=jnp.float32,
    ) / groups
    grad[...] = outer_grad.reshape(grad.shape)
    for way in range(2):
        block = base.at[around(zh, 2, zhs), way]
        wait(block, far_send, far_recv.at[2 + way])
    fresh = base[...] - outer_rate * (1 + momentum_rate) * grad[...]
    full[g, :, zl, y] = fresh.astype(jnp.bfloat16)

    def hop(axis, d, dy=0):
        return device(d, dy, 0, 0) if axis == 0 else device(0, dy, d, 0)

    def block(part, u, w, o):
        dg, dz = (u, w) if part == 0 else (w, u)
        return full.at[around(g, -dg, groups), :, around(zl, -dz, zls), y if o == 0 else 1 - y, part]

    froms = (0,) + AROUND

    def last(part, j, o):
        for way in range(2):
            if j % 2 == way:
                came = last_recv.at[part, j, o]
            else:
                came = end_recv
            copy(block(part, froms[j], 0, o), last_send, came, hop(1 - part, 1 - 2 * way)).start()

    def middle(j, o):
        for part in range(2):
            wait(block(part, froms[j], 0, o), mid_send, mid_recv.at[part, j - 1, o])
            last(part, j, o)

    def onward(j, o):
        for part in range(2):
            way = j % 2
            came = block(part, froms[j], 1 - 2 * way, o)
            wait(came, last_send, last_recv.at[part, j, o])
            copy(came, end_send, end_recv, hop(1 - part, 1 - 2 * way)).start()

    for dy in range(2):
        if dy:
            here = full.at[g, :, zl, y]
            copy(here, y_send, y_recv, device(0, 1, 0, 0)).start()
        for j, d in enumerate(AROUND):
            for part in range(2):
                copy(block(part, 0, 0, 0), mid_send, mid_recv.at[part, j, dy], hop(part, d, dy)).start()
    for part in range(2):
        last(part, 0, 0)
    moved = momentum_rate * momentum[...]
    own = grad.at[zh]
    for i in range(2):
        new_momentum[i * half : (i + 1) * half] = moved[i * half : (i + 1) * half] + own[i]
        new_master[i * half : (i + 1) * half] = mine[i] - outer_rate * (1 + momentum_rate) * own[i]
    for j in range(1, 4):
        middle(j, 0)
    wait(full.at[g, :, zl, 1 - y], y_send, y_recv)
    for part in range(2):
        last(part, 0, 1)
    for j in range(1, 4):
        middle(j, 1)
    wait_sent(incoming, sum_send)
    wait_sent(base.at[0:3], far_send)
    wait_sent(full.at[0, :, 0, 0], y_send)
    for o in range(2):
        for j in range(4):
            onward(j, o)
    wait_sent(full.at[0:3, :, 0], mid_send)
    wait_sent(full.at[0:2], last_send)
    wait(full.at[0:2], end_send, end_recv)
    wait_sent(full.at[0:1], end_send)


def store(*refs):
    sem = refs[-1]
    count = len(refs) // 2
    moves = [pltpu.make_async_copy(refs[i], refs[count + i], sem.at[i]) for i in range(count)]
    for move in moves:
        move.start()
    for move in moves:
        move.wait()


def shards(deltas, factor, master, momentum):
    groups = lax.axis_size("group")
    tensors = lax.axis_size("tensor")
    depth = lax.axis_size("shard") // 2
    rows, cols = master.shape
    rank = factor.shape[1]
    anywhere = pl.BlockSpec(memory_space=pl.ANY)
    vmem = pl.BlockSpec(memory_space=pltpu.VMEM)
    dma = pltpu.SemaphoreType.DMA
    zls = depth // 4
    full = (groups, 4, zls, 2, 2, rows // 2, cols)
    four = (4, 2, rows // 2, cols)
    results = pl.pallas_call(
        kernel,
        out_shape=(
            pltpu.VMEM(master.shape, jnp.float32),
            pltpu.VMEM(momentum.shape, jnp.float32),
            pltpu.VMEM(full, jnp.bfloat16),
        ),
        in_specs=[anywhere] * 4,
        out_specs=(vmem,) * 3,
        scratch_shapes=[
            pltpu.VMEM((groups, 4, rows, cols), jnp.bfloat16),
            pltpu.VMEM((rank, cols), jnp.bfloat16),
            pltpu.VMEM((rows, cols), jnp.float32),
            pltpu.VMEM((rows, cols), jnp.float32),
            pltpu.VMEM((groups, 2 * rows, 2 * rank), jnp.float32),
            pltpu.VMEM((groups * tensors - 1, 2 * rows, 2 * rank), jnp.float32),
            pltpu.VMEM(four, jnp.float32),
            pltpu.VMEM(four, jnp.float32),
            dma((4,)), dma, dma, dma, dma((4,)), dma, dma,
            dma, dma((2, 3, 2)), dma, dma((2, 4, 2)), dma, dma,
        ],
        compiler_params=pltpu.CompilerParams(collective_id=0, has_side_effects=True),
    )(deltas.reshape(groups, 4, zls, 2, rows, cols), factor.T, master, momentum)
    new_master, new_momentum, weights = pl.pallas_call(
        store,
        out_shape=tuple(jax.ShapeDtypeStruct(r.shape, r.dtype) for r in results),
        in_specs=[anywhere] * 3,
        out_specs=(anywhere,) * 3,
        scratch_shapes=[dma((3,))],
        compiler_params=pltpu.CompilerParams(vmem_limit_bytes=1 << 20),
    )(*results)
    return new_master, new_momentum, weights.reshape(groups * depth * 2 * rows, cols)


def solution(mesh):
    return jax.shard_map(
        shards,
        mesh=mesh,
        in_specs=(
            P("group", None, "tensor"),
            P("tensor", None),
            P(("group", "shard"), "tensor"),
            P(("group", "shard"), "tensor"),
        ),
        out_specs=(
            P(("group", "shard"), "tensor"),
            P(("group", "shard"), "tensor"),
            P(None, "tensor"),
        ),
        check_vma=False,
    )
```

```python
import jax
import jax.numpy as jnp
from jax import lax
from jax.experimental import pallas as pl
from jax.experimental.pallas import tpu as pltpu
from jax.sharding import PartitionSpec as P

momentum_rate = 0.9
outer_rate = 0.7
MESH = pl.DeviceIdType.MESH
AROUND = (1, -1, 2)


def kernel(
    deltas_ref, factor_ref, master_ref, momentum_ref,
    new_master, new_momentum, full,
    delta, factor, master, momentum, partial, incoming, base, grad,
    in_sem, sum_send, sum_recv, far_send, far_recv, y_send, y_recv,
    mid_send, mid_recv, last_send, last_recv, end_send, end_recv,
):
    groups, zls = full.shape[0], full.shape[3]
    zhs = full.shape[1] * full.shape[2]
    tensors = lax.axis_size("tensor")
    g, s, t = lax.axis_index("group"), lax.axis_index("shard"), lax.axis_index("tensor")
    z, y = s // 2, s % 2
    depth = zhs * zls
    rows = master.shape[0]
    half = rows // 2
    rank = factor.shape[0]

    def around(value, step, size):
        return lax.rem(value + step + size, size)

    def device(dg, dy, dz, dt):
        shard = around(z, dz, depth) * 2 + around(y, dy, 2)
        return (around(g, dg, groups), shard, around(t, dt, tensors))

    def place(dz):
        other = around(z, dz, depth)
        return other // zls, lax.rem(other, zls)

    zh, zl = place(0)
    loads = [
        pltpu.make_async_copy(master_ref, master, in_sem.at[0]),
        pltpu.make_async_copy(momentum_ref, momentum, in_sem.at[1]),
        pltpu.make_async_copy(deltas_ref.at[:, :, zl, y], delta, in_sem.at[2]),
        pltpu.make_async_copy(factor_ref, factor, in_sem.at[3]),
    ]
    for load in loads:
        load.start()

    sums = [(dg, dt) for dg in (2, 1, -1, 0) for dt in (2, 1, -1, 0) if dg or dt]
    peers = [(0, 0, dz, 0) for dz in (zls, -zls)]
    peers += [(0, dy, dz, 0) for dz in (2, -2, 1, -1) for dy in range(2)]
    peers += [(dg, 1, 0, 0) for dg in (2, 1, -1, 0)]
    peers += [(dg, 0, 0, dt) for dg, dt in sums]
    barrier = pltpu.get_barrier_semaphore()
    for peer in peers:
        pl.semaphore_signal(barrier, inc=1, device_id=device(*peer), device_id_type=MESH)

    loads[0].wait()
    loads[1].wait()
    start = master[...] - outer_rate * momentum_rate * momentum_rate * momentum[...]

    def rows_of(ref, step):
        other = around(zh, step, zhs)
        return ref.at[other // 2, other % 2]

    mine = rows_of(base, 0)
    mine[0] = start[:half]
    mine[1] = start[half:]
    loads[2].wait()
    loads[3].wait()
    span = zhs * rows
    part = lax.dot_general(
        delta[...].reshape(groups * span, delta.shape[-1]), factor[...], (((1,), (1,)), ((), ())),
        preferred_element_type=jnp.float32,
    )
    for i in range(groups):
        own = part[i * span : (i + 1) * span]
        partial[i] = jnp.concatenate([own[: span // 2], own[span // 2 :]], axis=1)

    pl.semaphore_wait(barrier, len(peers))

    def copy(block, send_sem, recv_sem, target, into=None):
        return pltpu.make_async_remote_copy(
            src_ref=block, dst_ref=block if into is None else into,
            send_sem=send_sem, recv_sem=recv_sem, device_id=target, device_id_type=MESH,
        )

    def wait(block, send_sem, recv_sem):
        copy(block, send_sem, recv_sem, device(0, 1, 0, 0)).wait_recv()

    def wait_sent(block, send_sem):
        copy(block, send_sem, end_recv, device(0, 1, 0, 0)).wait_send()

    def far(way, order, part):
        target = device(0, 0, zls * (1 - 2 * way), 0)
        return copy(part, far_send, far_recv.at[way, order], target)

    for order in range(2):
        for way in range(2):
            far(way, order, mine.at[(way + order) % 2]).start()
    for i, (dg, dt) in enumerate(sums):
        target = device(dg, 0, 0, dt)
        copy(partial.at[target[0]], sum_send, sum_recv, target, incoming.at[i]).start()
    for way in range(2):
        came = rows_of(base, 2 * way - 1).at[way]
        far(way, 0, came).wait_recv()
        far(way, 2, came).start()
    for way in range(2):
        far(way, 1, rows_of(base, 2 * way - 1).at[1 - way]).wait_recv()

    wait(incoming, sum_send, sum_recv)
    total = partial[g]
    for i in range(len(sums)):
        total = total + incoming[i]
    coefficients = jnp.concatenate([total[:, :rank], total[:, rank:]], axis=0)
    outer_grad = lax.dot_general(
        coefficients, factor[...].astype(jnp.float32), (((1,), (0,)), ((), ())),
        precision=lax.Precision.HIGHEST, preferred_element_type=jnp.float32,
    ) / groups
    grad[...] = outer_grad.reshape(grad.shape)

    def pair(k, dz=0):
        zh_of, zl_of = place(dz)
        return (zh_of + 1 - k) % 2, zl_of

    def hop(axis, d, dy=0):
        return device(d, dy, 0, 0) if axis == 0 else device(0, dy, d, 0)

    def block(part, u, w, k, o):
        dg, dz = (u, w) if part == 0 else (w, u)
        parity, zl_of = pair(k, -dz)
        return full.at[around(g, -dg, groups), :, parity, zl_of, y if o == 0 else 1 - y, part]

    froms = (0,) + AROUND

    def last(j, k, o, part):
        for way in range(2):
            came = last_recv.at[part, j, k, o] if j % 2 == way else end_recv
            copy(block(part, froms[j], 0, k, o), last_send, came, hop(1 - part, 1 - 2 * way)).start()

    def finish(k):
        parity = pair(k)[0]
        fresh = base[:, parity] - outer_rate * (1 + momentum_rate) * grad[:, parity]
        full[g, :, parity, zl, y] = fresh.astype(jnp.bfloat16)
        for dy in range(2):
            if dy:
                here = full.at[g, :, parity, zl, y]
                copy(here, y_send, y_recv.at[k], device(0, 1, 0, 0)).start()
            for j, d in enumerate(AROUND):
                for part in range(2):
                    copy(
                        block(part, 0, 0, k, 0), mid_send, mid_recv.at[part, j, k, dy], hop(part, d, dy)
                    ).start()
        for part in range(2):
            last(0, k, 0, part)

    def middle(j, k, o):
        for part in range(2):
            if j:
                wait(block(part, froms[j], 0, k, o), mid_send, mid_recv.at[part, j - 1, k, o])
            elif part == 0:
                wait(full.at[g, :, pair(k)[0], zl, 1 - y], y_send, y_recv.at[k])
            last(j, k, o, part)

    def onward(j, k, o):
        for part in range(2):
            way = j % 2
            came = block(part, froms[j], 1 - 2 * way, k, o)
            wait(came, last_send, last_recv.at[part, j, k, o])
            copy(came, end_send, end_recv, hop(1 - part, 1 - 2 * way)).start()

    finish(0)
    moved = momentum_rate * momentum[...]
    own = rows_of(grad, 0)
    for i in range(2):
        new_momentum[i * half : (i + 1) * half] = moved[i * half : (i + 1) * half] + own[i]
        new_master[i * half : (i + 1) * half] = mine[i] - outer_rate * (1 + momentum_rate) * own[i]
    for j, k, o in ((1, 0, 0), (2, 0, 0), (0, 0, 1)):
        middle(j, k, o)
    onward(0, 0, 0)
    middle(3, 0, 0)
    middle(1, 0, 1)
    for way in range(2):
        far(way, 2, rows_of(base, 2).at[way]).wait_recv()
    finish(1)
    onward(1, 0, 0)
    onward(2, 0, 0)
    middle(2, 0, 1)
    onward(0, 0, 1)
    middle(3, 0, 1)
    onward(3, 0, 0)
    onward(1, 0, 1)
    for j, k, o in ((1, 1, 0), (2, 1, 0), (0, 1, 1)):
        middle(j, k, o)
    onward(0, 1, 0)
    onward(2, 0, 1)
    middle(1, 1, 1)
    middle(2, 1, 1)
    onward(3, 0, 1)
    middle(3, 1, 0)
    onward(2, 1, 0)
    onward(1, 1, 0)
    onward(0, 1, 1)
    middle(3, 1, 1)
    onward(1, 1, 1)
    onward(2, 1, 1)
    onward(3, 1, 0)
    onward(3, 1, 1)
    wait_sent(incoming, sum_send)
    wait_sent(incoming.at[0:6], far_send)
    wait_sent(full.at[0, :, :, 0, 0], y_send)
    wait_sent(full.at[0:3, :, :, 0], mid_send)
    wait_sent(full.at[0:2], last_send)
    wait(full.at[0:2], end_send, end_recv)
    wait_sent(full.at[0:1], end_send)


def store(*refs):
    sem = refs[-1]
    count = len(refs) // 2
    moves = [pltpu.make_async_copy(refs[i], refs[count + i], sem.at[i]) for i in range(count)]
    for move in moves:
        move.start()
    for move in moves:
        move.wait()


def shards(deltas, factor, master, momentum):
    groups = lax.axis_size("group")
    tensors = lax.axis_size("tensor")
    depth = lax.axis_size("shard") // 2
    rows, cols = master.shape
    rank = factor.shape[1]
    anywhere = pl.BlockSpec(memory_space=pl.ANY)
    vmem = pl.BlockSpec(memory_space=pltpu.VMEM)
    dma = pltpu.SemaphoreType.DMA
    zls = depth // 4
    full = (groups, 2, 2, zls, 2, 2, rows // 2, cols)
    four = (2, 2, 2, rows // 2, cols)
    results = pl.pallas_call(
        kernel,
        out_shape=(
            pltpu.VMEM(master.shape, jnp.float32),
            pltpu.VMEM(momentum.shape, jnp.float32),
            pltpu.VMEM(full, jnp.bfloat16),
        ),
        in_specs=[anywhere] * 4,
        out_specs=(vmem,) * 3,
        scratch_shapes=[
            pltpu.VMEM((groups, 4, rows, cols), jnp.bfloat16),
            pltpu.VMEM((rank, cols), jnp.bfloat16),
            pltpu.VMEM((rows, cols), jnp.float32),
            pltpu.VMEM((rows, cols), jnp.float32),
            pltpu.VMEM((groups, 2 * rows, 2 * rank), jnp.float32),
            pltpu.VMEM((groups * tensors - 1, 2 * rows, 2 * rank), jnp.float32),
            pltpu.VMEM(four, jnp.float32),
            pltpu.VMEM(four, jnp.float32),
            dma((4,)), dma, dma, dma, dma((2, 3)), dma, dma((2,)),
            dma, dma((2, 3, 2, 2)), dma, dma((2, 4, 2, 2)), dma, dma,
        ],
        compiler_params=pltpu.CompilerParams(collective_id=0, has_side_effects=True),
    )(deltas.reshape(groups, 4, zls, 2, rows, cols), factor.T, master, momentum)
    new_master, new_momentum, weights = pl.pallas_call(
        store,
        out_shape=tuple(jax.ShapeDtypeStruct(r.shape, r.dtype) for r in results),
        in_specs=[anywhere] * 3,
        out_specs=(anywhere,) * 3,
        scratch_shapes=[dma((3,))],
        compiler_params=pltpu.CompilerParams(vmem_limit_bytes=1 << 20),
    )(*results)
    return new_master, new_momentum, weights.reshape(groups * depth * 2 * rows, cols)


def solution(mesh):
    return jax.shard_map(
        shards,
        mesh=mesh,
        in_specs=(
            P("group", None, "tensor"),
            P("tensor", None),
            P(("group", "shard"), "tensor"),
            P(("group", "shard"), "tensor"),
        ),
        out_specs=(
            P(("group", "shard"), "tensor"),
            P(("group", "shard"), "tensor"),
            P(None, "tensor"),
        ),
        check_vma=False,
    )
```

```python
import jax
import jax.numpy as jnp
from jax import lax
from jax.experimental import pallas as pl
from jax.experimental.pallas import tpu as pltpu
from jax.sharding import PartitionSpec as P

momentum_rate = 0.9
outer_rate = 0.7
MESH = pl.DeviceIdType.MESH
AROUND = (1, -1, 2)


def kernel(
    deltas_ref, factor_ref, master_ref, momentum_ref,
    new_master, new_momentum, full,
    delta, factor, master, momentum, partial, incoming, base, grad,
    in_sem, sum_send, sum_recv, far_send, far_recv, y_send, y_recv,
    mid_send, mid_recv, last_send, last_recv, end_send, end_recv,
):
    groups, zls = full.shape[0], full.shape[3]
    zhs = full.shape[1] * full.shape[2]
    tensors = lax.axis_size("tensor")
    g, s, t = lax.axis_index("group"), lax.axis_index("shard"), lax.axis_index("tensor")
    z, y = s // 2, s % 2
    depth = zhs * zls
    rows = master.shape[0]
    half = rows // 2
    rank = factor.shape[0]

    def around(value, step, size):
        return lax.rem(value + step + size, size)

    def device(dg, dy, dz, dt):
        shard = around(z, dz, depth) * 2 + around(y, dy, 2)
        return (around(g, dg, groups), shard, around(t, dt, tensors))

    def place(dz):
        other = around(z, dz, depth)
        return other // zls, lax.rem(other, zls)

    zh, zl = place(0)
    loads = [
        pltpu.make_async_copy(master_ref, master, in_sem.at[0]),
        pltpu.make_async_copy(momentum_ref, momentum, in_sem.at[1]),
        pltpu.make_async_copy(deltas_ref.at[:, :, zl, y], delta, in_sem.at[2]),
        pltpu.make_async_copy(factor_ref, factor, in_sem.at[3]),
    ]
    for load in loads:
        load.start()

    sums = [(dg, dt) for dg in (2, 1, -1, 0) for dt in (2, 1, -1, 0) if dg or dt]
    peers = [(0, 0, dz, 0) for dz in (zls, -zls)]
    peers += [(0, dy, dz, 0) for dz in (2, -2, 1, -1) for dy in range(2)]
    peers += [(dg, 1, 0, 0) for dg in (2, 1, -1, 0)]
    peers += [(dg, 0, 0, dt) for dg, dt in sums]
    barrier = pltpu.get_barrier_semaphore()
    for peer in peers:
        pl.semaphore_signal(barrier, inc=1, device_id=device(*peer), device_id_type=MESH)

    loads[0].wait()
    loads[1].wait()
    start = master[...] - outer_rate * momentum_rate * momentum_rate * momentum[...]

    def rows_of(ref, step):
        other = around(zh, step, zhs)
        return ref.at[other // 2, other % 2]

    mine = rows_of(base, 0)
    mine[0] = start[:half]
    mine[1] = start[half:]
    loads[2].wait()
    loads[3].wait()
    span = zhs * rows
    part = lax.dot_general(
        delta[...].reshape(groups * span, delta.shape[-1]), factor[...], (((1,), (1,)), ((), ())),
        preferred_element_type=jnp.float32,
    )
    for i in range(groups):
        own = part[i * span : (i + 1) * span]
        partial[i] = jnp.concatenate([own[: span // 2], own[span // 2 :]], axis=1)

    pl.semaphore_wait(barrier, len(peers))

    def copy(block, send_sem, recv_sem, target, into=None):
        return pltpu.make_async_remote_copy(
            src_ref=block, dst_ref=block if into is None else into,
            send_sem=send_sem, recv_sem=recv_sem, device_id=target, device_id_type=MESH,
        )

    def wait(block, send_sem, recv_sem):
        copy(block, send_sem, recv_sem, device(0, 1, 0, 0)).wait_recv()

    def wait_sent(block, send_sem):
        copy(block, send_sem, end_recv, device(0, 1, 0, 0)).wait_send()

    def far(way, order, part):
        target = device(0, 0, zls * (1 - 2 * way), 0)
        return copy(part, far_send, far_recv.at[way, order], target)

    for order in range(2):
        for way in range(2):
            far(way, order, mine.at[(way + order) % 2]).start()
    for i, (dg, dt) in enumerate(sums):
        target = device(dg, 0, 0, dt)
        copy(partial.at[target[0]], sum_send, sum_recv, target, incoming.at[i]).start()
    for way in range(2):
        came = rows_of(base, 2 * way - 1).at[way]
        far(way, 0, came).wait_recv()
        far(way, 2, came).start()
    for way in range(2):
        far(way, 1, rows_of(base, 2 * way - 1).at[1 - way]).wait_recv()

    wait(incoming, sum_send, sum_recv)
    total = partial[g]
    for i in range(len(sums)):
        total = total + incoming[i]
    coefficients = jnp.concatenate([total[:, :rank], total[:, rank:]], axis=0)
    outer_grad = lax.dot_general(
        coefficients, factor[...].astype(jnp.float32), (((1,), (0,)), ((), ())),
        precision=lax.Precision.HIGHEST, preferred_element_type=jnp.float32,
    ) / groups
    grad[...] = outer_grad.reshape(grad.shape)

    def pair(k, dz=0):
        zh_of, zl_of = place(dz)
        return (zh_of + 1 - k) % 2, zl_of

    def hop(axis, d, dy=0):
        return device(d, dy, 0, 0) if axis == 0 else device(0, dy, d, 0)

    def block(part, u, w, k, o):
        dg, dz = (u, w) if part == 0 else (w, u)
        parity, zl_of = pair(k, -dz)
        return full.at[around(g, -dg, groups), :, parity, zl_of, y if o == 0 else 1 - y, part]

    froms = (0,) + AROUND

    def last(j, k, o, part):
        for way in range(2):
            came = last_recv.at[part, j, k, o] if j % 2 == way else end_recv
            copy(block(part, froms[j], 0, k, o), last_send, came, hop(1 - part, 1 - 2 * way)).start()

    def finish(k):
        parity = pair(k)[0]
        fresh = base[:, parity] - outer_rate * (1 + momentum_rate) * grad[:, parity]
        full[g, :, parity, zl, y] = fresh.astype(jnp.bfloat16)
        for dy in range(2):
            if dy:
                here = full.at[g, :, parity, zl, y]
                copy(here, y_send, y_recv.at[k], device(0, 1, 0, 0)).start()
            for j, d in enumerate(AROUND):
                for part in range(2):
                    copy(
                        block(part, 0, 0, k, 0), mid_send, mid_recv.at[part, j, k, dy], hop(part, d, dy)
                    ).start()
        for part in range(2):
            last(0, k, 0, part)

    def middle(j, k, o):
        for part in range(2):
            if j:
                wait(block(part, froms[j], 0, k, o), mid_send, mid_recv.at[part, j - 1, k, o])
            elif part == 0:
                wait(full.at[g, :, pair(k)[0], zl, 1 - y], y_send, y_recv.at[k])
            last(j, k, o, part)

    def onward(j, k, o):
        for part in range(2):
            way = j % 2
            came = block(part, froms[j], 1 - 2 * way, k, o)
            wait(came, last_send, last_recv.at[part, j, k, o])
            copy(came, end_send, end_recv, hop(1 - part, 1 - 2 * way)).start()

    finish(0)
    moved = momentum_rate * momentum[...]
    own = rows_of(grad, 0)
    for i in range(2):
        new_momentum[i * half : (i + 1) * half] = moved[i * half : (i + 1) * half] + own[i]
        new_master[i * half : (i + 1) * half] = mine[i] - outer_rate * (1 + momentum_rate) * own[i]
    for way in range(2):
        far(way, 2, rows_of(base, 2).at[way]).wait_recv()
    finish(1)
    for j in (1, 2, 3):
        middle(j, 0, 0)
    for j in range(4):
        middle(j, 0, 1)
    for j in (1, 2, 3):
        middle(j, 1, 0)
    for j in range(4):
        middle(j, 1, 1)
    for j in range(4):
        onward(j, 0, 0)
    for j in range(4):
        onward(j, 0, 1)
    for j in range(4):
        onward(j, 1, 0)
    for j in range(4):
        onward(j, 1, 1)
    wait_sent(incoming, sum_send)
    wait_sent(incoming.at[0:6], far_send)
    wait_sent(full.at[0, :, :, 0, 0], y_send)
    wait_sent(full.at[0:3, :, :, 0], mid_send)
    wait_sent(full.at[0:2], last_send)
    wait(full.at[0:2], end_send, end_recv)
    wait_sent(full.at[0:1], end_send)


def store(*refs):
    sem = refs[-1]
    count = len(refs) // 2
    moves = [pltpu.make_async_copy(refs[i], refs[count + i], sem.at[i]) for i in range(count)]
    for move in moves:
        move.start()
    for move in moves:
        move.wait()


def shards(deltas, factor, master, momentum):
    groups = lax.axis_size("group")
    tensors = lax.axis_size("tensor")
    depth = lax.axis_size("shard") // 2
    rows, cols = master.shape
    rank = factor.shape[1]
    anywhere = pl.BlockSpec(memory_space=pl.ANY)
    vmem = pl.BlockSpec(memory_space=pltpu.VMEM)
    dma = pltpu.SemaphoreType.DMA
    zls = depth // 4
    full = (groups, 2, 2, zls, 2, 2, rows // 2, cols)
    four = (2, 2, 2, rows // 2, cols)
    results = pl.pallas_call(
        kernel,
        out_shape=(
            pltpu.VMEM(master.shape, jnp.float32),
            pltpu.VMEM(momentum.shape, jnp.float32),
            pltpu.VMEM(full, jnp.bfloat16),
        ),
        in_specs=[anywhere] * 4,
        out_specs=(vmem,) * 3,
        scratch_shapes=[
            pltpu.VMEM((groups, 4, rows, cols), jnp.bfloat16),
            pltpu.VMEM((rank, cols), jnp.bfloat16),
            pltpu.VMEM((rows, cols), jnp.float32),
            pltpu.VMEM((rows, cols), jnp.float32),
            pltpu.VMEM((groups, 2 * rows, 2 * rank), jnp.float32),
            pltpu.VMEM((groups * tensors - 1, 2 * rows, 2 * rank), jnp.float32),
            pltpu.VMEM(four, jnp.float32),
            pltpu.VMEM(four, jnp.float32),
            dma((4,)), dma, dma, dma, dma((2, 3)), dma, dma((2,)),
            dma, dma((2, 3, 2, 2)), dma, dma((2, 4, 2, 2)), dma, dma,
        ],
        compiler_params=pltpu.CompilerParams(collective_id=0, has_side_effects=True),
    )(deltas.reshape(groups, 4, zls, 2, rows, cols), factor.T, master, momentum)
    new_master, new_momentum, weights = pl.pallas_call(
        store,
        out_shape=tuple(jax.ShapeDtypeStruct(r.shape, r.dtype) for r in results),
        in_specs=[anywhere] * 3,
        out_specs=(anywhere,) * 3,
        scratch_shapes=[dma((3,))],
        compiler_params=pltpu.CompilerParams(vmem_limit_bytes=1 << 20),
    )(*results)
    return new_master, new_momentum, weights.reshape(groups * depth * 2 * rows, cols)


def solution(mesh):
    return jax.shard_map(
        shards,
        mesh=mesh,
        in_specs=(
            P("group", None, "tensor"),
            P("tensor", None),
            P(("group", "shard"), "tensor"),
            P(("group", "shard"), "tensor"),
        ),
        out_specs=(
            P(("group", "shard"), "tensor"),
            P(("group", "shard"), "tensor"),
            P(None, "tensor"),
        ),
        check_vma=False,
    )
```

```python
import jax
import jax.numpy as jnp
from jax import lax
from jax.experimental import pallas as pl
from jax.experimental.pallas import tpu as pltpu
from jax.sharding import PartitionSpec as P

momentum_rate = 0.9
outer_rate = 0.7
MESH = pl.DeviceIdType.MESH
AROUND = (1, -1, 2)


def kernel(
    deltas_ref, factor_ref, master_ref, momentum_ref,
    new_master, new_momentum, full,
    delta, factor, master, momentum, partial, incoming, base, grad,
    in_sem, sum_send, sum_recv, far_send, far_recv, y_send, y_recv,
    mid_send, mid_recv, last_send, last_recv, end_send, end_recv,
):
    groups, zls = full.shape[0], full.shape[3]
    zhs = full.shape[1] * full.shape[2]
    tensors = lax.axis_size("tensor")
    g, s, t = lax.axis_index("group"), lax.axis_index("shard"), lax.axis_index("tensor")
    z, y = s // 2, s % 2
    depth = zhs * zls
    rows = master.shape[0]
    half = rows // 2
    rank = factor.shape[0]

    def around(value, step, size):
        return lax.rem(value + step + size, size)

    def device(dg, dy, dz, dt):
        shard = around(z, dz, depth) * 2 + around(y, dy, 2)
        return (around(g, dg, groups), shard, around(t, dt, tensors))

    def place(dz):
        other = around(z, dz, depth)
        return other // zls, lax.rem(other, zls)

    zh, zl = place(0)
    loads = [
        pltpu.make_async_copy(master_ref, master, in_sem.at[0]),
        pltpu.make_async_copy(momentum_ref, momentum, in_sem.at[1]),
        pltpu.make_async_copy(deltas_ref.at[:, :, zl, y], delta, in_sem.at[2]),
        pltpu.make_async_copy(factor_ref, factor, in_sem.at[3]),
    ]
    for load in loads:
        load.start()

    sums = [(dg, dt) for dg in (2, 1, -1, 0) for dt in (2, 1, -1, 0) if dg or dt]
    peers = [(0, 0, dz, 0) for dz in (zls, -zls)]
    peers += [(0, dy, dz, 0) for dz in (2, -2, 1, -1) for dy in range(2)]
    peers += [(dg, 1, 0, 0) for dg in (2, 1, -1, 0)]
    peers += [(dg, 0, 0, dt) for dg, dt in sums]
    barrier = pltpu.get_barrier_semaphore()
    for peer in peers:
        pl.semaphore_signal(barrier, inc=1, device_id=device(*peer), device_id_type=MESH)

    loads[0].wait()
    loads[1].wait()
    start = master[...] - outer_rate * momentum_rate * momentum_rate * momentum[...]

    def rows_of(ref, step):
        other = around(zh, step, zhs)
        return ref.at[other // 2, other % 2]

    mine = rows_of(base, 0)
    mine[0] = start[:half]
    mine[1] = start[half:]
    loads[2].wait()
    loads[3].wait()
    span = zhs * rows
    part = lax.dot_general(
        delta[...].reshape(groups * span, delta.shape[-1]), factor[...], (((1,), (1,)), ((), ())),
        preferred_element_type=jnp.float32,
    )
    for i in range(groups):
        own = part[i * span : (i + 1) * span]
        partial[i] = jnp.concatenate([own[: span // 2], own[span // 2 :]], axis=1)

    pl.semaphore_wait(barrier, len(peers))

    def copy(block, send_sem, recv_sem, target, into=None):
        return pltpu.make_async_remote_copy(
            src_ref=block, dst_ref=block if into is None else into,
            send_sem=send_sem, recv_sem=recv_sem, device_id=target, device_id_type=MESH,
        )

    def wait(block, send_sem, recv_sem):
        copy(block, send_sem, recv_sem, device(0, 1, 0, 0)).wait_recv()

    def wait_sent(block, send_sem):
        copy(block, send_sem, end_recv, device(0, 1, 0, 0)).wait_send()

    def far(way, order, part):
        target = device(0, 0, zls * (1 - 2 * way), 0)
        return copy(part, far_send, far_recv.at[way, order], target)

    for order in range(2):
        for way in range(2):
            far(way, order, mine.at[(way + order) % 2]).start()
    for i, (dg, dt) in enumerate(sums):
        target = device(dg, 0, 0, dt)
        copy(partial.at[target[0]], sum_send, sum_recv, target, incoming.at[i]).start()
    for way in range(2):
        came = rows_of(base, 2 * way - 1).at[way]
        far(way, 0, came).wait_recv()
        far(way, 2, came).start()
    wait(incoming, sum_send, sum_recv)
    total = partial[g]
    for i in range(len(sums)):
        total = total + incoming[i]
    coefficients = jnp.concatenate([total[:, :rank], total[:, rank:]], axis=0)
    outer_grad = lax.dot_general(
        coefficients, factor[...].astype(jnp.float32), (((1,), (0,)), ((), ())),
        precision=lax.Precision.HIGHEST, preferred_element_type=jnp.float32,
    ) / groups
    grad[...] = outer_grad.reshape(grad.shape)
    for way in range(2):
        far(way, 1, rows_of(base, 2 * way - 1).at[1 - way]).wait_recv()

    def spots(k, dz, index):
        zh_of, zl_of = place(dz)
        far_of = around(zh_of, 2, zhs)
        single = zh_of if k == 0 else far_of
        found = [full.at[(index[0], single // 2, single % 2, zl_of) + index[1:]]]
        if k == 0:
            found.append(full.at[(index[0], slice(None), 1 - zh_of % 2, zl_of) + index[1:]])
        return found

    def amount(k, *index):
        return full.at[(0, 0, 0, slice(0, 3) if k == 0 else 0) + index]

    def hop(axis, d, dy=0):
        return device(d, dy, 0, 0) if axis == 0 else device(0, dy, d, 0)

    def block(part, u, w, k, o):
        dg, dz = (u, w) if part == 0 else (w, u)
        return spots(k, -dz, (around(g, -dg, groups), y if o == 0 else 1 - y, part))

    froms = (0,) + AROUND

    def last(j, k, o, part):
        for way in range(2):
            came = last_recv.at[part, j, k, o] if j % 2 == way else end_recv
            for piece in block(part, froms[j], 0, k, o):
                copy(piece, last_send, came, hop(1 - part, 1 - 2 * way)).start()

    def finish(k):
        for step in (0, 1, -1) if k == 0 else (2,):
            other = around(zh, step, zhs)
            fresh = rows_of(base, step)[...] - outer_rate * (1 + momentum_rate) * rows_of(grad, step)[...]
            full[g, other // 2, other % 2, zl, y] = fresh.astype(jnp.bfloat16)
        for dy in range(2):
            if dy:
                for piece in spots(k, 0, (g, y)):
                    copy(piece, y_send, y_recv.at[k], device(0, 1, 0, 0)).start()
            for j, d in enumerate(AROUND):
                for part in range(2):
                    for piece in block(part, 0, 0, k, 0):
                        copy(piece, mid_send, mid_recv.at[part, j, k, dy], hop(part, d, dy)).start()
        for part in range(2):
            last(0, k, 0, part)

    def middle(j, k, o):
        for part in range(2):
            if j:
                wait(amount(k, 0, 0), mid_send, mid_recv.at[part, j - 1, k, o])
            elif part == 0:
                wait(amount(k, 0), y_send, y_recv.at[k])
            last(j, k, o, part)

    def onward(j, k, o):
        for part in range(2):
            way = j % 2
            wait(amount(k, 0, 0), last_send, last_recv.at[part, j, k, o])
            for piece in block(part, froms[j], 1 - 2 * way, k, o):
                copy(piece, end_send, end_recv, hop(1 - part, 1 - 2 * way)).start()

    finish(0)
    moved = momentum_rate * momentum[...]
    own = rows_of(grad, 0)
    for i in range(2):
        new_momentum[i * half : (i + 1) * half] = moved[i * half : (i + 1) * half] + own[i]
        new_master[i * half : (i + 1) * half] = mine[i] - outer_rate * (1 + momentum_rate) * own[i]
    for way in range(2):
        far(way, 2, rows_of(base, 2).at[way]).wait_recv()
    finish(1)
    for j in (1, 2, 3):
        middle(j, 0, 0)
    for j in range(4):
        middle(j, 0, 1)
    for j in (1, 2, 3):
        middle(j, 1, 0)
    for j in range(4):
        middle(j, 1, 1)
    for j in range(4):
        onward(j, 0, 0)
    for j in range(4):
        onward(j, 0, 1)
    for j in range(4):
        onward(j, 1, 0)
    for j in range(4):
        onward(j, 1, 1)
    wait_sent(incoming, sum_send)
    wait_sent(incoming.at[0:6], far_send)
    wait_sent(full.at[0, :, :, 0, 0], y_send)
    wait_sent(full.at[0:3, :, :, 0], mid_send)
    wait_sent(full.at[0:2], last_send)
    wait(full.at[0:2], end_send, end_recv)
    wait_sent(full.at[0:1], end_send)


def store(*refs):
    sem = refs[-1]
    count = len(refs) // 2
    moves = [pltpu.make_async_copy(refs[i], refs[count + i], sem.at[i]) for i in range(count)]
    for move in moves:
        move.start()
    for move in moves:
        move.wait()


def shards(deltas, factor, master, momentum):
    groups = lax.axis_size("group")
    tensors = lax.axis_size("tensor")
    depth = lax.axis_size("shard") // 2
    rows, cols = master.shape
    rank = factor.shape[1]
    anywhere = pl.BlockSpec(memory_space=pl.ANY)
    vmem = pl.BlockSpec(memory_space=pltpu.VMEM)
    dma = pltpu.SemaphoreType.DMA
    zls = depth // 4
    full = (groups, 2, 2, zls, 2, 2, rows // 2, cols)
    four = (2, 2, 2, rows // 2, cols)
    results = pl.pallas_call(
        kernel,
        out_shape=(
            pltpu.VMEM(master.shape, jnp.float32),
            pltpu.VMEM(momentum.shape, jnp.float32),
            pltpu.VMEM(full, jnp.bfloat16),
        ),
        in_specs=[anywhere] * 4,
        out_specs=(vmem,) * 3,
        scratch_shapes=[
            pltpu.VMEM((groups, 4, rows, cols), jnp.bfloat16),
            pltpu.VMEM((rank, cols), jnp.bfloat16),
            pltpu.VMEM((rows, cols), jnp.float32),
            pltpu.VMEM((rows, cols), jnp.float32),
            pltpu.VMEM((groups, 2 * rows, 2 * rank), jnp.float32),
            pltpu.VMEM((groups * tensors - 1, 2 * rows, 2 * rank), jnp.float32),
            pltpu.VMEM(four, jnp.float32),
            pltpu.VMEM(four, jnp.float32),
            dma((4,)), dma, dma, dma, dma((2, 3)), dma, dma((2,)),
            dma, dma((2, 3, 2, 2)), dma, dma((2, 4, 2, 2)), dma, dma,
        ],
        compiler_params=pltpu.CompilerParams(collective_id=0, has_side_effects=True),
    )(deltas.reshape(groups, 4, zls, 2, rows, cols), factor.T, master, momentum)
    new_master, new_momentum, weights = pl.pallas_call(
        store,
        out_shape=tuple(jax.ShapeDtypeStruct(r.shape, r.dtype) for r in results),
        in_specs=[anywhere] * 3,
        out_specs=(anywhere,) * 3,
        scratch_shapes=[dma((3,))],
        compiler_params=pltpu.CompilerParams(vmem_limit_bytes=1 << 20),
    )(*results)
    return new_master, new_momentum, weights.reshape(groups * depth * 2 * rows, cols)


def solution(mesh):
    return jax.shard_map(
        shards,
        mesh=mesh,
        in_specs=(
            P("group", None, "tensor"),
            P("tensor", None),
            P(("group", "shard"), "tensor"),
            P(("group", "shard"), "tensor"),
        ),
        out_specs=(
            P(("group", "shard"), "tensor"),
            P(("group", "shard"), "tensor"),
            P(None, "tensor"),
        ),
        check_vma=False,
    )
```

```python
import jax
import jax.numpy as jnp
from jax import lax
from jax.experimental import pallas as pl
from jax.experimental.pallas import tpu as pltpu
from jax.sharding import PartitionSpec as P

momentum_rate = 0.9
outer_rate = 0.7
MESH = pl.DeviceIdType.MESH
AROUND = (1, -1, 2)


def kernel(
    deltas_ref, factor_ref, master_ref, momentum_ref,
    new_master, new_momentum, full,
    delta, factor, master, momentum, partial, incoming, base, grad,
    in_sem, sum_send, sum_recv, far_send, far_recv, y_send, y_recv,
    mid_send, mid_recv, last_send, last_recv, end_send, end_recv,
):
    groups, zls = full.shape[0], full.shape[3]
    zhs = full.shape[1] * full.shape[2]
    tensors = lax.axis_size("tensor")
    g, s, t = lax.axis_index("group"), lax.axis_index("shard"), lax.axis_index("tensor")
    z, y = s // 2, s % 2
    depth = zhs * zls
    rows = master.shape[0]
    half = rows // 2
    rank = factor.shape[0]

    def around(value, step, size):
        return lax.rem(value + step + size, size)

    def device(dg, dy, dz, dt):
        shard = around(z, dz, depth) * 2 + around(y, dy, 2)
        return (around(g, dg, groups), shard, around(t, dt, tensors))

    def place(dz):
        other = around(z, dz, depth)
        return other // zls, lax.rem(other, zls)

    zh, zl = place(0)
    loads = [
        pltpu.make_async_copy(master_ref, master, in_sem.at[0]),
        pltpu.make_async_copy(momentum_ref, momentum, in_sem.at[1]),
        pltpu.make_async_copy(deltas_ref.at[:, :, zl, y], delta, in_sem.at[2]),
        pltpu.make_async_copy(factor_ref, factor, in_sem.at[3]),
    ]
    sums = [(dg, dt) for dg in (2, 1, -1, 0) for dt in (2, 1, -1, 0) if dg or dt]
    peers = [(0, 0, dz, 0) for dz in (zls, -zls)]
    peers += [(0, dy, dz, 0) for dz in (2, -2, 1, -1) for dy in range(2)]
    peers += [(dg, 1, 0, 0) for dg in (2, 1, -1, 0)]
    peers += [(dg, 0, 0, dt) for dg, dt in sums]
    barrier = pltpu.get_barrier_semaphore()
    for i, peer in enumerate(peers):
        pl.semaphore_signal(barrier, inc=1, device_id=device(*peer), device_id_type=MESH)
        if i == 1:
            for load in loads:
                load.start()

    loads[0].wait()
    loads[1].wait()
    start = master[...] - outer_rate * momentum_rate * momentum_rate * momentum[...]

    def rows_of(ref, step):
        other = around(zh, step, zhs)
        return ref.at[other // 2, other % 2]

    mine = rows_of(base, 0)
    mine[0] = start[:half]
    mine[1] = start[half:]
    loads[2].wait()
    loads[3].wait()
    span = zhs * rows
    part = lax.dot_general(
        delta[...].reshape(groups * span, delta.shape[-1]), factor[...], (((1,), (1,)), ((), ())),
        preferred_element_type=jnp.float32,
    )
    for i in range(groups):
        own = part[i * span : (i + 1) * span]
        partial[i] = jnp.concatenate([own[: span // 2], own[span // 2 :]], axis=1)

    pl.semaphore_wait(barrier, len(peers))

    def copy(block, send_sem, recv_sem, target, into=None):
        return pltpu.make_async_remote_copy(
            src_ref=block, dst_ref=block if into is None else into,
            send_sem=send_sem, recv_sem=recv_sem, device_id=target, device_id_type=MESH,
        )

    def wait(block, send_sem, recv_sem):
        copy(block, send_sem, recv_sem, device(0, 1, 0, 0)).wait_recv()

    def wait_sent(block, send_sem):
        copy(block, send_sem, end_recv, device(0, 1, 0, 0)).wait_send()

    def far(way, order, part):
        target = device(0, 0, zls * (1 - 2 * way), 0)
        return copy(part, far_send, far_recv.at[way, order], target)

    for order in range(2):
        for way in range(2):
            far(way, order, mine.at[(way + order) % 2]).start()
    for i, (dg, dt) in enumerate(sums):
        target = device(dg, 0, 0, dt)
        copy(partial.at[target[0]], sum_send, sum_recv, target, incoming.at[i]).start()
    for way in range(2):
        came = rows_of(base, 2 * way - 1).at[way]
        far(way, 0, came).wait_recv()
        far(way, 2, came).start()
    wait(incoming, sum_send, sum_recv)
    total = partial[g]
    for i in range(len(sums)):
        total = total + incoming[i]
    coefficients = jnp.concatenate([total[:, :rank], total[:, rank:]], axis=0)
    outer_grad = lax.dot_general(
        coefficients, factor[...].astype(jnp.float32), (((1,), (0,)), ((), ())),
        precision=lax.Precision.HIGHEST, preferred_element_type=jnp.float32,
    ) / groups
    grad[...] = outer_grad.reshape(grad.shape)

    def spots(k, dz, index):
        zh_of, zl_of = place(dz)
        far_of = around(zh_of, 2, zhs)
        single = zh_of if k == 0 else far_of
        found = [full.at[(index[0], single // 2, single % 2, zl_of) + index[1:]]]
        if k == 0:
            found.append(full.at[(index[0], slice(None), 1 - zh_of % 2, zl_of) + index[1:]])
        return found

    def amount(k, *index):
        return full.at[(0, 0, 0, slice(0, 3) if k == 0 else 0) + index]

    def hop(axis, d, dy=0):
        return device(d, dy, 0, 0) if axis == 0 else device(0, dy, d, 0)

    def block(part, u, w, k, o):
        dg, dz = (u, w) if part == 0 else (w, u)
        return spots(k, -dz, (around(g, -dg, groups), y if o == 0 else 1 - y, part))

    froms = (0,) + AROUND

    def last(j, k, o, part, picked=slice(None)):
        for way in range(2):
            came = last_recv.at[part, j, k, o] if j % 2 == way else end_recv
            for piece in block(part, froms[j], 0, k, o)[picked]:
                copy(piece, last_send, came, hop(1 - part, 1 - 2 * way)).start()

    def finish(k, steps, picked):
        for step in steps:
            other = around(zh, step, zhs)
            fresh = rows_of(base, step)[...] - outer_rate * (1 + momentum_rate) * rows_of(grad, step)[...]
            full[g, other // 2, other % 2, zl, y] = fresh.astype(jnp.bfloat16)
        for dy in range(2):
            if dy:
                for piece in spots(k, 0, (g, y))[picked]:
                    copy(piece, y_send, y_recv.at[k], device(0, 1, 0, 0)).start()
            for j, d in enumerate(AROUND):
                for part in range(2):
                    for piece in block(part, 0, 0, k, 0)[picked]:
                        copy(piece, mid_send, mid_recv.at[part, j, k, dy], hop(part, d, dy)).start()
        for part in range(2):
            last(0, k, 0, part, picked)

    def middle(j, k, o):
        for part in range(2):
            if j:
                wait(amount(k, 0, 0), mid_send, mid_recv.at[part, j - 1, k, o])
            elif part == 0:
                wait(amount(k, 0), y_send, y_recv.at[k])
            last(j, k, o, part)

    def onward(j, k, o):
        for part in range(2):
            way = j % 2
            wait(amount(k, 0, 0), last_send, last_recv.at[part, j, k, o])
            for piece in block(part, froms[j], 1 - 2 * way, k, o):
                copy(piece, end_send, end_recv, hop(1 - part, 1 - 2 * way)).start()

    finish(0, (0,), slice(0, 1))
    for way in range(2):
        far(way, 1, rows_of(base, 2 * way - 1).at[1 - way]).wait_recv()
    finish(0, (1, -1), slice(1, 2))
    moved = momentum_rate * momentum[...]
    own = rows_of(grad, 0)
    for i in range(2):
        new_momentum[i * half : (i + 1) * half] = moved[i * half : (i + 1) * half] + own[i]
        new_master[i * half : (i + 1) * half] = mine[i] - outer_rate * (1 + momentum_rate) * own[i]
    for way in range(2):
        far(way, 2, rows_of(base, 2).at[way]).wait_recv()
    finish(1, (2,), slice(0, 1))
    for j in (1, 2, 3):
        middle(j, 0, 0)
    for j in range(4):
        middle(j, 0, 1)
    for j in (1, 2, 3):
        middle(j, 1, 0)
    for j in range(4):
        middle(j, 1, 1)
    for j in range(4):
        onward(j, 0, 0)
    for j in range(4):
        onward(j, 0, 1)
    for j in range(4):
        onward(j, 1, 0)
    for j in range(4):
        onward(j, 1, 1)
    wait_sent(incoming, sum_send)
    wait_sent(incoming.at[0:6], far_send)
    wait_sent(full.at[0, :, :, 0, 0], y_send)
    wait_sent(full.at[0:3, :, :, 0], mid_send)
    wait_sent(full.at[0:2], last_send)
    wait(full.at[0:2], end_send, end_recv)
    wait_sent(full.at[0:1], end_send)


def store(*refs):
    sem = refs[-1]
    count = len(refs) // 2
    moves = [pltpu.make_async_copy(refs[i], refs[count + i], sem.at[i]) for i in range(count - 1)]
    for i in range(refs[count - 1].shape[0]):
        moves.append(pltpu.make_async_copy(refs[count - 1].at[i], refs[-2].at[i], sem.at[count - 1 + i]))
    for move in moves:
        move.start()
    for move in moves:
        move.wait()


def shards(deltas, factor, master, momentum):
    groups = lax.axis_size("group")
    tensors = lax.axis_size("tensor")
    depth = lax.axis_size("shard") // 2
    rows, cols = master.shape
    rank = factor.shape[1]
    anywhere = pl.BlockSpec(memory_space=pl.ANY)
    vmem = pl.BlockSpec(memory_space=pltpu.VMEM)
    dma = pltpu.SemaphoreType.DMA
    zls = depth // 4
    full = (groups, 2, 2, zls, 2, 2, rows // 2, cols)
    four = (2, 2, 2, rows // 2, cols)
    results = pl.pallas_call(
        kernel,
        out_shape=(
            pltpu.VMEM(master.shape, jnp.float32),
            pltpu.VMEM(momentum.shape, jnp.float32),
            pltpu.VMEM(full, jnp.bfloat16),
        ),
        in_specs=[anywhere] * 4,
        out_specs=(vmem,) * 3,
        scratch_shapes=[
            pltpu.VMEM((groups, 4, rows, cols), jnp.bfloat16),
            pltpu.VMEM((rank, cols), jnp.bfloat16),
            pltpu.VMEM((rows, cols), jnp.float32),
            pltpu.VMEM((rows, cols), jnp.float32),
            pltpu.VMEM((groups, 2 * rows, 2 * rank), jnp.float32),
            pltpu.VMEM((groups * tensors - 1, 2 * rows, 2 * rank), jnp.float32),
            pltpu.VMEM(four, jnp.float32),
            pltpu.VMEM(four, jnp.float32),
            dma((4,)), dma, dma, dma, dma((2, 3)), dma, dma((2,)),
            dma, dma((2, 3, 2, 2)), dma, dma((2, 4, 2, 2)), dma, dma,
        ],
        compiler_params=pltpu.CompilerParams(collective_id=0, has_side_effects=True),
    )(deltas.reshape(groups, 4, zls, 2, rows, cols), factor.T, master, momentum)
    new_master, new_momentum, weights = pl.pallas_call(
        store,
        out_shape=tuple(jax.ShapeDtypeStruct(r.shape, r.dtype) for r in results),
        in_specs=[anywhere] * 3,
        out_specs=(anywhere,) * 3,
        scratch_shapes=[dma((2 + groups,))],
        compiler_params=pltpu.CompilerParams(vmem_limit_bytes=1 << 20),
    )(*results)
    return new_master, new_momentum, weights.reshape(groups * depth * 2 * rows, cols)


def solution(mesh):
    return jax.shard_map(
        shards,
        mesh=mesh,
        in_specs=(
            P("group", None, "tensor"),
            P("tensor", None),
            P(("group", "shard"), "tensor"),
            P(("group", "shard"), "tensor"),
        ),
        out_specs=(
            P(("group", "shard"), "tensor"),
            P(("group", "shard"), "tensor"),
            P(None, "tensor"),
        ),
        check_vma=False,
    )
```

```python
import jax
import jax.numpy as jnp
from jax import lax
from jax.experimental import pallas as pl
from jax.experimental.pallas import tpu as pltpu
from jax.sharding import PartitionSpec as P

momentum_rate = 0.9
outer_rate = 0.7
MESH = pl.DeviceIdType.MESH
AROUND = (1, -1, 2)


def kernel(
    deltas_ref, factor_ref, master_ref, momentum_ref,
    new_master, new_momentum, full,
    delta, factor, master, momentum, partial, incoming, base, grad,
    in_sem, sum_send, sum_recv, far_send, far_recv, y_send, y_recv,
    mid_send, mid_recv, last_send, last_recv, end_send, end_recv,
):
    groups, zls = full.shape[0], full.shape[3]
    zhs = full.shape[1] * full.shape[2]
    tensors = lax.axis_size("tensor")
    g, s, t = lax.axis_index("group"), lax.axis_index("shard"), lax.axis_index("tensor")
    z, y = s // 2, s % 2
    depth = zhs * zls
    rows = master.shape[0]
    half = rows // 2
    rank = factor.shape[0]

    def around(value, step, size):
        return lax.rem(value + step + size, size)

    def device(dg, dy, dz, dt):
        shard = around(z, dz, depth) * 2 + around(y, dy, 2)
        return (around(g, dg, groups), shard, around(t, dt, tensors))

    def place(dz):
        other = around(z, dz, depth)
        return other // zls, lax.rem(other, zls)

    zh, zl = place(0)
    loads = [
        pltpu.make_async_copy(master_ref, master, in_sem.at[0]),
        pltpu.make_async_copy(momentum_ref, momentum, in_sem.at[1]),
        pltpu.make_async_copy(deltas_ref.at[:, :, zl, y], delta, in_sem.at[2]),
        pltpu.make_async_copy(factor_ref, factor, in_sem.at[3]),
    ]
    for load in loads:
        load.start()

    sums = [(dg, dt) for dg in (2, 1, -1, 0) for dt in (2, 1, -1, 0) if dg or dt]
    peers = [(0, 0, dz, 0) for dz in (zls, -zls)]
    peers += [(0, dy, dz, 0) for dz in (2, -2, 1, -1) for dy in range(2)]
    peers += [(dg, 1, 0, 0) for dg in (2, 1, -1, 0)]
    peers += [(dg, 0, 0, dt) for dg, dt in sums]
    barrier = pltpu.get_barrier_semaphore()
    for peer in peers:
        pl.semaphore_signal(barrier, inc=1, device_id=device(*peer), device_id_type=MESH)

    loads[0].wait()
    loads[1].wait()
    start = master[...] - outer_rate * momentum_rate * momentum_rate * momentum[...]

    def rows_of(ref, step):
        other = around(zh, step, zhs)
        return ref.at[other // 2, other % 2]

    mine = rows_of(base, 0)
    mine[0] = start[:half]
    mine[1] = start[half:]
    loads[2].wait()
    loads[3].wait()
    span = zhs * rows
    part = lax.dot_general(
        delta[...].reshape(groups * span, delta.shape[-1]), factor[...], (((1,), (1,)), ((), ())),
        preferred_element_type=jnp.float32,
    )
    for i in range(groups):
        own = part[i * span : (i + 1) * span]
        partial[i] = jnp.concatenate([own[: span // 2], own[span // 2 :]], axis=1)

    pl.semaphore_wait(barrier, len(peers))

    def copy(block, send_sem, recv_sem, target, into=None):
        return pltpu.make_async_remote_copy(
            src_ref=block, dst_ref=block if into is None else into,
            send_sem=send_sem, recv_sem=recv_sem, device_id=target, device_id_type=MESH,
        )

    def wait(block, send_sem, recv_sem):
        copy(block, send_sem, recv_sem, device(0, 1, 0, 0)).wait_recv()

    def wait_sent(block, send_sem):
        copy(block, send_sem, end_recv, device(0, 1, 0, 0)).wait_send()

    def far(way, order, part):
        target = device(0, 0, zls * (1 - 2 * way), 0)
        return copy(part, far_send, far_recv.at[way, order], target)

    for order in range(2):
        for way in range(2):
            far(way, order, mine.at[(way + order) % 2]).start()
    for i, (dg, dt) in enumerate(sums):
        target = device(dg, 0, 0, dt)
        copy(partial.at[target[0]], sum_send, sum_recv, target, incoming.at[i]).start()
    for way in range(2):
        came = rows_of(base, 2 * way - 1).at[way]
        far(way, 0, came).wait_recv()
        far(way, 2, came).start()
    wait(incoming, sum_send, sum_recv)
    total = partial[g]
    for i in range(len(sums)):
        total = total + incoming[i]
    coefficients = jnp.concatenate([total[:, :rank], total[:, rank:]], axis=0)
    outer_grad = lax.dot_general(
        coefficients, factor[...].astype(jnp.float32), (((1,), (0,)), ((), ())),
        precision=lax.Precision.HIGHEST, preferred_element_type=jnp.float32,
    ) / groups
    grad[...] = outer_grad.reshape(grad.shape)

    def spots(k, dz, index):
        zh_of, zl_of = place(dz)
        far_of = around(zh_of, 2, zhs)
        single = zh_of if k == 0 else far_of
        found = [full.at[(index[0], single // 2, single % 2, zl_of) + index[1:]]]
        if k == 0:
            found.append(full.at[(index[0], slice(None), 1 - zh_of % 2, zl_of) + index[1:]])
        return found

    def amount(k, *index):
        return full.at[(0, 0, 0, slice(0, 3) if k == 0 else 0) + index]

    def hop(axis, d, dy=0):
        return device(d, dy, 0, 0) if axis == 0 else device(0, dy, d, 0)

    def block(part, u, w, k, o):
        dg, dz = (u, w) if part == 0 else (w, u)
        return spots(k, -dz, (around(g, -dg, groups), y if o == 0 else 1 - y, part))

    froms = (0,) + AROUND

    def last(j, k, o, part, picked=slice(None)):
        for way in range(2):
            came = last_recv.at[part, j, k, o] if j % 2 == way else end_recv
            for piece in block(part, froms[j], 0, k, o)[picked]:
                copy(piece, last_send, came, hop(1 - part, 1 - 2 * way)).start()

    def finish(k, steps, picked):
        for step in steps:
            other = around(zh, step, zhs)
            fresh = rows_of(base, step)[...] - outer_rate * (1 + momentum_rate) * rows_of(grad, step)[...]
            full[g, other // 2, other % 2, zl, y] = fresh.astype(jnp.bfloat16)
        for dy in range(2):
            if dy:
                for piece in spots(k, 0, (g, y))[picked]:
                    copy(piece, y_send, y_recv.at[k], device(0, 1, 0, 0)).start()
            for j, d in enumerate(AROUND):
                for part in range(2):
                    for piece in block(part, 0, 0, k, 0)[picked]:
                        copy(piece, mid_send, mid_recv.at[part, j, k, dy], hop(part, d, dy)).start()
        for part in range(2):
            last(0, k, 0, part, picked)

    def middle(j, k, o):
        for part in range(2):
            if j:
                wait(amount(k, 0, 0), mid_send, mid_recv.at[part, j - 1, k, o])
            elif part == 0:
                wait(amount(k, 0), y_send, y_recv.at[k])
            last(j, k, o, part)

    def onward(j, k, o):
        for part in range(2):
            way = j % 2
            wait(amount(k, 0, 0), last_send, last_recv.at[part, j, k, o])
            for piece in block(part, froms[j], 1 - 2 * way, k, o):
                copy(piece, end_send, end_recv, hop(1 - part, 1 - 2 * way)).start()

    finish(0, (0,), slice(0, 1))
    for way in range(2):
        far(way, 1, rows_of(base, 2 * way - 1).at[1 - way]).wait_recv()
    finish(0, (1, -1), slice(1, 2))
    moved = momentum_rate * momentum[...]
    own = rows_of(grad, 0)
    for i in range(2):
        new_momentum[i * half : (i + 1) * half] = moved[i * half : (i + 1) * half] + own[i]
        new_master[i * half : (i + 1) * half] = mine[i] - outer_rate * (1 + momentum_rate) * own[i]
    for way in range(2):
        far(way, 2, rows_of(base, 2).at[way]).wait_recv()
    finish(1, (2,), slice(0, 1))
    for j in (1, 2, 3):
        middle(j, 0, 0)
    for j in range(4):
        middle(j, 0, 1)
    for j in (1, 2, 3):
        middle(j, 1, 0)
    for j in range(4):
        middle(j, 1, 1)
    for j in range(4):
        onward(j, 0, 0)
    for j in range(4):
        onward(j, 0, 1)
    for j in range(4):
        onward(j, 1, 0)
    for j in range(4):
        onward(j, 1, 1)
    wait_sent(incoming, sum_send)
    wait_sent(incoming.at[0:6], far_send)
    wait_sent(full.at[0, :, :, 0, 0], y_send)
    wait_sent(full.at[0:3, :, :, 0], mid_send)
    wait_sent(full.at[0:2], last_send)
    wait(full.at[0:2], end_send, end_recv)
    wait_sent(full.at[0:1], end_send)


def store(*refs):
    sem = refs[-1]
    count = len(refs) // 2
    moves = [pltpu.make_async_copy(refs[i], refs[count + i], sem.at[i]) for i in range(count)]
    for move in moves:
        move.start()
    for move in moves:
        move.wait()


def shards(deltas, factor, master, momentum):
    groups = lax.axis_size("group")
    tensors = lax.axis_size("tensor")
    depth = lax.axis_size("shard") // 2
    rows, cols = master.shape
    rank = factor.shape[1]
    anywhere = pl.BlockSpec(memory_space=pl.ANY)
    vmem = pl.BlockSpec(memory_space=pltpu.VMEM)
    dma = pltpu.SemaphoreType.DMA
    zls = depth // 4
    full = (groups, 2, 2, zls, 2, 2, rows // 2, cols)
    four = (2, 2, 2, rows // 2, cols)
    results = pl.pallas_call(
        kernel,
        out_shape=(
            pltpu.VMEM(master.shape, jnp.float32),
            pltpu.VMEM(momentum.shape, jnp.float32),
            pltpu.VMEM(full, jnp.bfloat16),
        ),
        in_specs=[anywhere] * 4,
        out_specs=(vmem,) * 3,
        scratch_shapes=[
            pltpu.VMEM((groups, 4, rows, cols), jnp.bfloat16),
            pltpu.VMEM((rank, cols), jnp.bfloat16),
            pltpu.VMEM((rows, cols), jnp.float32),
            pltpu.VMEM((rows, cols), jnp.float32),
            pltpu.VMEM((groups, 2 * rows, 2 * rank), jnp.float32),
            pltpu.VMEM((groups * tensors - 1, 2 * rows, 2 * rank), jnp.float32),
            pltpu.VMEM(four, jnp.float32),
            pltpu.VMEM(four, jnp.float32),
            dma((4,)), dma, dma, dma, dma((2, 3)), dma, dma((2,)),
            dma, dma((2, 3, 2, 2)), dma, dma((2, 4, 2, 2)), dma, dma,
        ],
        compiler_params=pltpu.CompilerParams(collective_id=0, has_side_effects=True),
    )(deltas.reshape(groups, 4, zls, 2, rows, cols), factor.T, master, momentum)
    new_master, new_momentum, weights = pl.pallas_call(
        store,
        out_shape=tuple(jax.ShapeDtypeStruct(r.shape, r.dtype) for r in results),
        in_specs=[anywhere] * 3,
        out_specs=(anywhere,) * 3,
        scratch_shapes=[dma((3,))],
        compiler_params=pltpu.CompilerParams(vmem_limit_bytes=1 << 20),
    )(*results)
    return new_master, new_momentum, weights.reshape(groups * depth * 2 * rows, cols)


def solution(mesh):
    return jax.shard_map(
        shards,
        mesh=mesh,
        in_specs=(
            P("group", None, "tensor"),
            P("tensor", None),
            P(("group", "shard"), "tensor"),
            P(("group", "shard"), "tensor"),
        ),
        out_specs=(
            P(("group", "shard"), "tensor"),
            P(("group", "shard"), "tensor"),
            P(None, "tensor"),
        ),
        check_vma=False,
    )
```
